128 devices in a mesh: row: 8 (over x, core), col: 16 (over y, z).
Axes of the slice: x: 4, y: 4, z: 4, core: 2. Of those that a mesh axis runs over, the one named last changes fastest.
Arguments:
- front_blocks: float32 [16, 1024, 8, 2048], P(None, 'row', None, 'col'), may hold values from -2.5 to 10.5, as said below
- child_updates: bfloat16 [2, 12, 1024, 6, 2048], P(None, None, 'row', None, 'col'), may hold values from -0.2 to 2.2, as said below
- child_map: int32 [2, 96], replicated, may hold values from 0 to 127, as said below
Outputs:
- factored: float32 [16, 1024, 8, 2048], P(None, 'row', None, 'col')
The draws below stay inside these ranges and needn't reach their ends.
Inputs may be any that keep to these rules, and one draw needn't show every extreme that they name: `child_map`: for each child, block a * 16 + j (0 <= j < 16) lands in front block h_a * 16 + ((s_a - j) mod 16), with 6 distinct h_a below 8 and s_a = (s + q_a) mod 16, q a permutation of 0 .. 5. Hence along col one device sends at most 1 of a child's column blocks to one device, along row at most 2 of its row blocks, and both bounds are reached in every draw. `front_blocks`: symmetric positive definite. `child_updates`: each child update is symmetric.
All inputs are finite; a program needn't handle non-finite values.
Results may differ from the reference program's by a relative error of at most 0.0003.
Values may be sent and summed in bfloat16 or wider, within the bound.
A program may use at most 192 MiB of HBM per device.

```python
import math
import jax
import jax.numpy as jnp
from jax import lax

F = 16384
C = 12288
BLK = 128
PW = 256
PANELS = 2
PROW = 8
PCOL = 16
CB = 96
SROW = 16
SCOL = 8
KROW = 12
KCOL = 6
PD = 512


def symmetric_part(key, order, diag_low, diag_high):
    noise_key, diag_key = jax.random.split(key)
    noise = jnp.clip(jax.random.normal(noise_key, (order, order), jnp.float32), -4.0, 4.0)
    diag_values = jax.random.uniform(diag_key, (order,), jnp.float32, diag_low, diag_high)
    scale = 0.4 / math.sqrt(order)
    matrix = (noise + noise.T) * (scale / math.sqrt(2.0))
    positions = jnp.arange(order)
    return matrix.at[positions, positions].add(diag_values)


def draw_front_blocks(key, part):
    inner = max(F // 16, 128)
    factor_key, diag_key = jax.random.split(key)
    coupling = jnp.clip(jax.random.normal(factor_key, (F, inner), jnp.float32), -4.0, 4.0)
    diag_values = jax.random.uniform(diag_key, (F,), jnp.float32, 1.0, 3.0)
    coupling = coupling * (2.0 / math.sqrt(inner))
    gram = jnp.dot(coupling, coupling.T, precision=lax.Precision.HIGHEST, preferred_element_type=jnp.float32)
    gram = 0.5 * (gram + gram.T)
    positions = jnp.arange(F)
    matrix = gram.at[positions, positions].add(diag_values)
    return matrix.reshape(SROW, BLK * PROW, SCOL, BLK * PCOL)


def draw_child_updates(key, part):
    stacked = jnp.stack([symmetric_part(jax.random.fold_in(key, 11 + child_no), C, 1.0, 2.0) for child_no in range(2)])
    return stacked.reshape(2, KROW, BLK * PROW, KCOL, BLK * PCOL).astype(jnp.bfloat16)


def draw_child_map(key, part):
    rows_out = []
    for child_no in range(2):
        child_key = jax.random.fold_in(key, 101 + child_no)
        home_key, order_key, base_key = jax.random.split(child_key, 3)
        home_list = jax.random.permutation(home_key, SCOL)[:KCOL].astype(jnp.int32)
        order_list = jax.random.permutation(order_key, KCOL).astype(jnp.int32)
        base_shift = jax.random.randint(base_key, (), 0, PCOL, dtype=jnp.int32)
        shifts = (base_shift + order_list) % PCOL
        lanes = jnp.arange(PCOL, dtype=jnp.int32)
        block_list = home_list[:, None] * PCOL + (shifts[:, None] - lanes[None, :] + PCOL) % PCOL
        rows_out.append(block_list.reshape(CB))
    return jnp.stack(rows_out).astype(jnp.int32)


def setup_inputs(seed: int = 0) -> dict:
    seeds = jax.random.split(jax.random.key(seed), 4)
    front_blocks = draw_front_blocks(jax.random.fold_in(seeds[3], 71), 0)
    child_updates = draw_child_updates(jax.random.fold_in(seeds[3], 71), 0)
    child_map = draw_child_map(jax.random.fold_in(seeds[3], 71), 0)
    return {"front_blocks": front_blocks, "child_updates": child_updates, "child_map": child_map}


def reference(front_blocks, child_updates, child_map):
    matrix = front_blocks.reshape(F, F)
    offsets = jnp.arange(BLK, dtype=jnp.int32)
    children = child_updates.reshape(2, C, C)
    for child_no in range(2):
        index_list = (child_map[child_no][:, None] * BLK + offsets[None, :]).reshape(C).astype(jnp.int32)
        matrix = matrix.at[index_list[:, None], index_list[None, :]].add(children[child_no].astype(jnp.float32))
    row_ids = jnp.arange(F, dtype=jnp.int32)
    factors = []
    for panel_no in range(PANELS):
        first_col = panel_no * PW
        finish = first_col + PW
        factor = jnp.linalg.cholesky(matrix[first_col:finish, first_col:finish])
        solved = lax.linalg.triangular_solve(factor, matrix[:, first_col:finish], left_side=False, lower=True, transpose_a=True)
        lower_part = jnp.where(row_ids[:, None] >= finish, solved, jnp.zeros_like(solved))
        lower_part = lower_part.at[first_col:finish].set(factor)
        matrix = matrix - jnp.dot(lower_part.astype(jnp.float32), lower_part.T.astype(jnp.float32), precision=lax.Precision.HIGHEST, preferred_element_type=jnp.float32)
        factors.append(lower_part)
    result = matrix.at[:, :PD].set(jnp.concatenate(factors, axis=1))
    result = result.at[:PD, PD:].set(jnp.zeros((PD, F - PD), result.dtype))
    return result.reshape(SROW, BLK * PROW, SCOL, BLK * PCOL)
```

```python
import jax
import jax.numpy as jnp
from jax import lax
from jax.sharding import PartitionSpec as P

PW = 256
PANELS = 2
PD = 512
HI = lax.Precision.HIGHEST


def decode_map(child_map, lanes):
    base = child_map[:, ::lanes]
    home = base // lanes
    shift = base % lanes
    groups = base.shape[1]
    prev = (shift - 1) % lanes
    has_prev = jnp.any(prev[:, :, None] == shift[:, None, :], axis=2)
    start = jnp.sum(jnp.where(has_prev, 0, shift), axis=1)
    order = (shift - start[:, None]) % lanes
    picks = order[:, :, None] == jnp.arange(groups)[None, None, :]
    inv = jnp.sum(jnp.where(picks, jnp.arange(groups)[None, :, None], 0), axis=1)
    return home, shift, start, inv


def routed(packets, axis, devices, start):
    groups = len(packets)

    def branch(sigma):
        def run(*pk):
            return tuple(
                lax.ppermute(
                    pk[q], axis, [(j, (sigma + q - j) % devices) for j in range(devices)]
                )
                for q in range(groups)
            )

        return run

    return lax.switch(start % devices, [branch(sg) for sg in range(devices)], *packets)


def spread_pieces(piece, axis, owners, devices, pieces_axis):
    parts = devices // owners
    size = piece.shape[pieces_axis] // parts
    me = lax.axis_index(axis)
    sub = lax.slice_in_dim(piece, 0, size, axis=pieces_axis)
    for m in range(1, parts):
        part = lax.slice_in_dim(piece, m * size, (m + 1) * size, axis=pieces_axis)
        got = lax.ppermute(part, axis, [(k, m * owners + k) for k in range(owners)])
        sub = jnp.where(me // owners == m, got, sub)
    return lax.all_gather(sub, axis, axis=0, tiled=False), parts, size


def on_device(front_blocks, child_updates, child_map, row_count, col_count):
    row_index = lax.axis_index("row")
    col_index = lax.axis_index("col")
    slots_r, tile, slots_c, _ = front_blocks.shape
    child_count, kr_count, _, kc_count, _ = child_updates.shape
    home, shift, start, inv = decode_map(child_map, col_count)
    groups = home.shape[1]

    dense = []
    for i in range(child_count):
        with jax.named_scope("child_route_cols"):
            x = child_updates[i].reshape(kr_count, tile, kc_count * tile)
            col_packets = [
                lax.dynamic_slice_in_dim(x, inv[i, q] * tile, tile, axis=2) for q in range(groups)
            ]
            got = routed(col_packets, "col", col_count, start[i])
            y = jnp.stack(got, axis=2)
        with jax.named_scope("child_route_rows"):
            row_packets = [
                lax.dynamic_slice_in_dim(y, inv[i, q] * 2, 2, axis=0) for q in range(groups)
            ]
            got = routed(row_packets, "row", row_count, start[i])
            z = jnp.stack(got, axis=0).reshape(groups * 2, tile, groups, tile)
        with jax.named_scope("child_place"):
            qs = jnp.arange(groups)
            a_of = inv[i]
            s_of = shift[i, a_of]
            h_of = home[i, a_of]
            src = (start[i] + qs - row_index) % row_count
            per_home = col_count // row_count
            first = ((s_of - src) % col_count) // row_count
            row_slot = jnp.stack(
                [per_home * h_of + first, per_home * h_of + 1 - first], axis=1
            ).reshape(-1)
            col_slot = h_of
            row_src = jnp.sum(
                jnp.where(
                    row_slot[None, :] == jnp.arange(slots_r)[:, None],
                    jnp.arange(groups * 2)[None, :] + 1,
                    0,
                ),
                axis=1,
            ) - 1
            row_src = jnp.where(row_src < 0, groups * 2, row_src)
            col_src = jnp.sum(
                jnp.where(
                    col_slot[None, :] == jnp.arange(slots_c)[:, None],
                    jnp.arange(groups)[None, :] + 1,
                    0,
                ),
                axis=1,
            ) - 1
            col_src = jnp.where(col_src < 0, groups, col_src)
            zp = jnp.concatenate([z, jnp.zeros((1, tile, groups, tile), z.dtype)], axis=0)
            zp = jnp.take(zp, row_src, axis=0)
            zp = jnp.concatenate([zp, jnp.zeros((slots_r, tile, 1, tile), z.dtype)], axis=2)
            dense.append(jnp.take(zp, col_src, axis=2))

    with jax.named_scope("assemble"):
        assembled = front_blocks
        for d in dense:
            assembled = assembled + d.astype(jnp.float32)
        height = slots_r * tile
        breadth = slots_c * tile
        a2 = assembled.reshape(height, breadth)

    local_rows = jnp.arange(height, dtype=jnp.int32)
    row_global = (local_rows // tile * row_count + row_index) * tile + local_rows % tile
    local_cols = jnp.arange(breadth, dtype=jnp.int32)
    col_global = (local_cols // tile * col_count + col_index) * tile + local_cols % tile
    owners = PD // tile

    with jax.named_scope("gather_panel_rows"):
        g, parts, size = spread_pieces(a2[:, 0:tile], "col", owners, col_count, 0)
        g = g.reshape(parts, owners, size, tile).transpose(0, 2, 1, 3)
        g_rows = g.reshape(height, PD)
    with jax.named_scope("gather_panel_cols"):
        g, parts, size = spread_pieces(a2[0:tile, :], "row", owners, row_count, 0)
        g = g.reshape(parts, owners, size, breadth).transpose(1, 0, 2, 3)
        g_cols = g.reshape(PD, breadth)
    with jax.named_scope("gather_diagonal"):
        g, parts, size = spread_pieces(g_rows[0:tile, :], "row", owners, row_count, 0)
        g = g.reshape(parts, owners, size, PD).transpose(1, 0, 2, 3)
        diag = g.reshape(PD, PD)

    with jax.named_scope("factor_diagonal"):
        eye = jnp.eye(PW, dtype=jnp.float32)
        l11 = jnp.linalg.cholesky(diag[0:PW, 0:PW])
        w0 = lax.linalg.triangular_solve(l11, eye, left_side=True, lower=True).T
        l21 = jnp.dot(diag[PW:PD, 0:PW], w0, precision=HI)
        d22 = diag[PW:PD, PW:PD] - jnp.dot(l21, l21.T, precision=HI)
        l22 = jnp.linalg.cholesky(d22)
        w1 = lax.linalg.triangular_solve(l22, eye, left_side=True, lower=True).T

    def panel_rows(block, gidx):
        s0 = jnp.dot(block[:, 0:PW], w0, precision=HI)
        p0 = jnp.where(
            (gidx >= PW)[:, None], s0, jnp.take(l11, jnp.clip(gidx, 0, PW - 1), axis=0)
        )
        a1 = block[:, PW:PD] - jnp.dot(p0, l21.T, precision=HI)
        s1 = jnp.dot(a1, w1, precision=HI)
        in1 = (gidx >= PW) & (gidx < PD)
        p1 = jnp.where(
            (gidx >= PD)[:, None],
            s1,
            jnp.where(in1[:, None], jnp.take(l22, jnp.clip(gidx - PW, 0, PW - 1), axis=0), 0.0),
        )
        return jnp.concatenate([p0, p1], axis=1)

    with jax.named_scope("panel_factors"):
        pr = panel_rows(g_rows, row_global)
        pc = panel_rows(g_cols.T, col_global)

    with jax.named_scope("trailing_update"):
        out = a2 - jnp.dot(pr, pc.T, precision=HI)
        own = lax.dynamic_slice_in_dim(pr, jnp.minimum(col_index, owners - 1) * tile, tile, axis=1)
        first = jnp.where(col_index < owners, own, out[:, 0:tile])
        out = out.at[:, 0:tile].set(first)
        upper = (row_global[:, None] < PD) & (col_global[None, :] >= PD)
        out = jnp.where(upper, 0.0, out)
    return out.reshape(slots_r, tile, slots_c, tile)


def solution(mesh):
    placed = (P(None, "row", None, "col"), P(None, None, "row", None, "col"), P())
    row_count = mesh.shape["row"]
    col_count = mesh.shape["col"]

    def body(front_blocks, child_updates, child_map):
        return on_device(front_blocks, child_updates, child_map, row_count, col_count)

    return jax.shard_map(
        body,
        mesh=mesh,
        in_specs=placed,
        out_specs=P(None, "row", None, "col"),
        check_vma=False,
    )
```

```python
import functools

import jax
import jax.numpy as jnp
from jax import lax
from jax.experimental import pallas as pl
from jax.experimental.pallas import tpu as pltpu
from jax.sharding import PartitionSpec as P

PW = 256
PANELS = 2
PD = 512
HI = lax.Precision.HIGHEST
MESH = pl.DeviceIdType.MESH


def decode_map(child_map, lanes):
    base = child_map[:, ::lanes]
    home = base // lanes
    shift = base % lanes
    groups = base.shape[1]
    prev = (shift - 1) % lanes
    has_prev = jnp.any(prev[:, :, None] == shift[:, None, :], axis=2)
    start = jnp.sum(jnp.where(has_prev, 0, shift), axis=1)
    order = (shift - start[:, None]) % lanes
    picks = order[:, :, None] == jnp.arange(groups)[None, None, :]
    inv = jnp.sum(jnp.where(picks, jnp.arange(groups)[None, :, None], 0), axis=1)
    return home, shift, start, inv


def route_kernel(axis, devices, sigma, groups, pk_ref, out_ref, send_sem, recv_sem):
    me = lax.axis_index(axis)
    row_at = lax.axis_index("row")
    col_at = lax.axis_index("col")

    def where_to(partner):
        return (partner, col_at) if axis == "row" else (row_at, partner)

    partners = [lax.rem(sigma + q - me + devices, devices) for q in range(groups)]
    barrier = pltpu.get_barrier_semaphore()
    for q in range(groups):

        @pl.when(partners[q] != me)
        def _():
            pl.semaphore_signal(barrier, 1, device_id=where_to(partners[q]), device_id_type=MESH)

    peers = sum((p != me).astype(jnp.int32) for p in partners)
    pl.semaphore_wait(barrier, peers)

    remote = []
    local = []
    for q in range(groups):
        remote.append(
            pltpu.make_async_remote_copy(
                src_ref=pk_ref.at[q],
                dst_ref=out_ref.at[q],
                send_sem=send_sem.at[q],
                recv_sem=recv_sem.at[q],
                device_id=where_to(partners[q]),
                device_id_type=MESH,
            )
        )
        local.append(pltpu.make_async_copy(pk_ref.at[q], out_ref.at[q], recv_sem.at[q]))
    for q in range(groups):

        @pl.when(partners[q] != me)
        def _():
            remote[q].start()

        @pl.when(partners[q] == me)
        def _():
            local[q].start()

    for q in range(groups):

        @pl.when(partners[q] != me)
        def _():
            remote[q].wait()

        @pl.when(partners[q] == me)
        def _():
            local[q].wait()


def route_call(packets, axis, devices, sigma, base_id):
    groups = packets.shape[0]
    return pl.pallas_call(
        functools.partial(route_kernel, axis, devices, sigma, groups),
        out_shape=jax.ShapeDtypeStruct(packets.shape, packets.dtype),
        in_specs=[pl.BlockSpec(memory_space=pl.ANY)],
        out_specs=pl.BlockSpec(memory_space=pl.ANY),
        scratch_shapes=[pltpu.SemaphoreType.DMA((groups,)), pltpu.SemaphoreType.DMA((groups,))],
        compiler_params=pltpu.CompilerParams(collective_id=base_id + sigma, has_side_effects=True),
        name=f"route_{axis}_{sigma}",
    )(packets)


def routed(packets, axis, devices, start, base_id):
    branches = [
        functools.partial(route_call, axis=axis, devices=devices, sigma=sg, base_id=base_id)
        for sg in range(devices)
    ]
    return lax.switch(start % devices, branches, packets)


def spread_pieces(piece, axis, owners, devices, pieces_axis):
    parts = devices // owners
    size = piece.shape[pieces_axis] // parts
    me = lax.axis_index(axis)
    sub = lax.slice_in_dim(piece, 0, size, axis=pieces_axis)
    for m in range(1, parts):
        part = lax.slice_in_dim(piece, m * size, (m + 1) * size, axis=pieces_axis)
        got = lax.ppermute(part, axis, [(k, m * owners + k) for k in range(owners)])
        sub = jnp.where(me // owners == m, got, sub)
    return lax.all_gather(sub, axis, axis=0, tiled=False), parts, size


def on_device(front_blocks, child_updates, child_map, row_count, col_count):
    row_index = lax.axis_index("row")
    col_index = lax.axis_index("col")
    slots_r, tile, slots_c, _ = front_blocks.shape
    child_count, kr_count, _, kc_count, _ = child_updates.shape
    home, shift, start, inv = decode_map(child_map, col_count)
    groups = home.shape[1]

    dense = []
    for i in range(child_count):
        with jax.named_scope("child_route_cols"):
            x = child_updates[i].reshape(kr_count, tile, kc_count * tile)
            col_packets = jnp.stack(
                [lax.dynamic_slice_in_dim(x, inv[i, q] * tile, tile, axis=2) for q in range(groups)]
            )
            got = routed(col_packets, "col", col_count, start[i], 0)
            y = jnp.moveaxis(got, 0, 2)
        with jax.named_scope("child_route_rows"):
            row_packets = jnp.stack(
                [lax.dynamic_slice_in_dim(y, inv[i, q] * 2, 2, axis=0) for q in range(groups)]
            )
            got = routed(row_packets, "row", row_count, start[i], col_count)
            z = got.reshape(groups * 2, tile, groups, tile)
        with jax.named_scope("child_place"):
            qs = jnp.arange(groups)
            a_of = inv[i]
            s_of = shift[i, a_of]
            h_of = home[i, a_of]
            src = (start[i] + qs - row_index) % row_count
            per_home = col_count // row_count
            first = ((s_of - src) % col_count) // row_count
            row_slot = jnp.stack(
                [per_home * h_of + first, per_home * h_of + 1 - first], axis=1
            ).reshape(-1)
            col_slot = h_of
            row_src = jnp.sum(
                jnp.where(
                    row_slot[None, :] == jnp.arange(slots_r)[:, None],
                    jnp.arange(groups * 2)[None, :] + 1,
                    0,
                ),
                axis=1,
            ) - 1
            row_src = jnp.where(row_src < 0, groups * 2, row_src)
            col_src = jnp.sum(
                jnp.where(
                    col_slot[None, :] == jnp.arange(slots_c)[:, None],
                    jnp.arange(groups)[None, :] + 1,
                    0,
                ),
                axis=1,
            ) - 1
            col_src = jnp.where(col_src < 0, groups, col_src)
            zp = jnp.concatenate([z, jnp.zeros((1, tile, groups, tile), z.dtype)], axis=0)
            zp = jnp.take(zp, row_src, axis=0)
            zp = jnp.concatenate([zp, jnp.zeros((slots_r, tile, 1, tile), z.dtype)], axis=2)
            dense.append(jnp.take(zp, col_src, axis=2))

    with jax.named_scope("assemble"):
        assembled = front_blocks
        for d in dense:
            assembled = assembled + d.astype(jnp.float32)
        height = slots_r * tile
        breadth = slots_c * tile
        a2 = assembled.reshape(height, breadth)

    local_rows = jnp.arange(height, dtype=jnp.int32)
    row_global = (local_rows // tile * row_count + row_index) * tile + local_rows % tile
    local_cols = jnp.arange(breadth, dtype=jnp.int32)
    col_global = (local_cols // tile * col_count + col_index) * tile + local_cols % tile
    owners = PD // tile

    with jax.named_scope("gather_panel_rows"):
        g, parts, size = spread_pieces(a2[:, 0:tile], "col", owners, col_count, 0)
        g = g.reshape(parts, owners, size, tile).transpose(0, 2, 1, 3)
        g_rows = g.reshape(height, PD)
    with jax.named_scope("gather_panel_cols"):
        g, parts, size = spread_pieces(a2[0:tile, :], "row", owners, row_count, 0)
        g = g.reshape(parts, owners, size, breadth).transpose(1, 0, 2, 3)
        g_cols = g.reshape(PD, breadth)
    with jax.named_scope("gather_diagonal"):
        g, parts, size = spread_pieces(g_rows[0:tile, :], "row", owners, row_count, 0)
        g = g.reshape(parts, owners, size, PD).transpose(1, 0, 2, 3)
        diag = g.reshape(PD, PD)

    with jax.named_scope("factor_diagonal"):
        eye = jnp.eye(PW, dtype=jnp.float32)
        l11 = jnp.linalg.cholesky(diag[0:PW, 0:PW])
        w0 = lax.linalg.triangular_solve(l11, eye, left_side=True, lower=True).T
        l21 = jnp.dot(diag[PW:PD, 0:PW], w0, precision=HI)
        d22 = diag[PW:PD, PW:PD] - jnp.dot(l21, l21.T, precision=HI)
        l22 = jnp.linalg.cholesky(d22)
        w1 = lax.linalg.triangular_solve(l22, eye, left_side=True, lower=True).T

    def panel_rows(block, gidx):
        s0 = jnp.dot(block[:, 0:PW], w0, precision=HI)
        p0 = jnp.where(
            (gidx >= PW)[:, None], s0, jnp.take(l11, jnp.clip(gidx, 0, PW - 1), axis=0)
        )
        a1 = block[:, PW:PD] - jnp.dot(p0, l21.T, precision=HI)
        s1 = jnp.dot(a1, w1, precision=HI)
        in1 = (gidx >= PW) & (gidx < PD)
        p1 = jnp.where(
            (gidx >= PD)[:, None],
            s1,
            jnp.where(in1[:, None], jnp.take(l22, jnp.clip(gidx - PW, 0, PW - 1), axis=0), 0.0),
        )
        return jnp.concatenate([p0, p1], axis=1)

    with jax.named_scope("panel_factors"):
        pr = panel_rows(g_rows, row_global)
        pc = panel_rows(g_cols.T, col_global)

    with jax.named_scope("trailing_update"):
        out = a2 - jnp.dot(pr, pc.T, precision=HI)
        own = lax.dynamic_slice_in_dim(pr, jnp.minimum(col_index, owners - 1) * tile, tile, axis=1)
        first = jnp.where(col_index < owners, own, out[:, 0:tile])
        out = out.at[:, 0:tile].set(first)
        upper = (row_global[:, None] < PD) & (col_global[None, :] >= PD)
        out = jnp.where(upper, 0.0, out)
    return out.reshape(slots_r, tile, slots_c, tile)


def solution(mesh):
    placed = (P(None, "row", None, "col"), P(None, None, "row", None, "col"), P())
    row_count = mesh.shape["row"]
    col_count = mesh.shape["col"]

    def body(front_blocks, child_updates, child_map):
        return on_device(front_blocks, child_updates, child_map, row_count, col_count)

    return jax.shard_map(
        body,
        mesh=mesh,
        in_specs=placed,
        out_specs=P(None, "row", None, "col"),
        check_vma=False,
    )
```

```python
import functools

import jax
import jax.numpy as jnp
from jax import lax
from jax.experimental import pallas as pl
from jax.experimental.pallas import tpu as pltpu
from jax.sharding import PartitionSpec as P

PW = 256
PANELS = 2
PD = 512
HI = lax.Precision.HIGHEST
MESH = pl.DeviceIdType.MESH


def decode_map(child_map, lanes):
    base = child_map[:, ::lanes]
    home = base // lanes
    shift = base % lanes
    groups = base.shape[1]
    prev = (shift - 1) % lanes
    has_prev = jnp.any(prev[:, :, None] == shift[:, None, :], axis=2)
    start = jnp.sum(jnp.where(has_prev, 0, shift), axis=1)
    order = (shift - start[:, None]) % lanes
    picks = order[:, :, None] == jnp.arange(groups)[None, None, :]
    inv = jnp.sum(jnp.where(picks, jnp.arange(groups)[None, :, None], 0), axis=1)
    return home, shift, start, inv


def route_kernel(sigma, groups, row_count, col_count, pk_ref, out_ref, send_sem, recv_sem):
    row_at = lax.axis_index("row")
    col_at = lax.axis_index("col")
    sig_r = sigma % row_count
    targets = []
    for qr in range(groups):
        to_row = lax.rem(sig_r + qr - row_at + row_count, row_count)
        for qc in range(groups):
            to_col = lax.rem(sigma + qc - col_at + col_count, col_count)
            mine = (to_row == row_at) & (to_col == col_at)
            targets.append((qr, qc, to_row, to_col, mine))
    barrier = pltpu.get_barrier_semaphore()
    for qr, qc, to_row, to_col, mine in targets:

        @pl.when(jnp.logical_not(mine))
        def _():
            pl.semaphore_signal(barrier, 1, device_id=(to_row, to_col), device_id_type=MESH)

    peers = sum(jnp.logical_not(t[4]).astype(jnp.int32) for t in targets)
    pl.semaphore_wait(barrier, peers)

    copies = []
    for n, (qr, qc, to_row, to_col, mine) in enumerate(targets):
        remote = pltpu.make_async_remote_copy(
            src_ref=pk_ref.at[qr, qc],
            dst_ref=out_ref.at[qr, qc],
            send_sem=send_sem.at[n],
            recv_sem=recv_sem.at[n],
            device_id=(to_row, to_col),
            device_id_type=MESH,
        )
        local = pltpu.make_async_copy(pk_ref.at[qr, qc], out_ref.at[qr, qc], recv_sem.at[n])
        copies.append((remote, local, mine))

        @pl.when(jnp.logical_not(mine))
        def _():
            remote.start()

        @pl.when(mine)
        def _():
            local.start()

    for remote, local, mine in copies:

        @pl.when(jnp.logical_not(mine))
        def _():
            remote.wait()

        @pl.when(mine)
        def _():
            local.wait()


def route_call(packets, sigma, row_count, col_count):
    groups = packets.shape[0]
    count = groups * groups
    return pl.pallas_call(
        functools.partial(route_kernel, sigma, groups, row_count, col_count),
        out_shape=jax.ShapeDtypeStruct(packets.shape, packets.dtype),
        in_specs=[pl.BlockSpec(memory_space=pl.ANY)],
        out_specs=pl.BlockSpec(memory_space=pl.ANY),
        scratch_shapes=[pltpu.SemaphoreType.DMA((count,)), pltpu.SemaphoreType.DMA((count,))],
        compiler_params=pltpu.CompilerParams(collective_id=sigma, has_side_effects=True),
        name=f"route_{sigma}",
    )(packets)


def routed(packets, start, row_count, col_count):
    branches = [
        functools.partial(route_call, sigma=sg, row_count=row_count, col_count=col_count)
        for sg in range(col_count)
    ]
    return lax.switch(start % col_count, branches, packets)


def spread_pieces(piece, axis, owners, devices, pieces_axis):
    parts = devices // owners
    size = piece.shape[pieces_axis] // parts
    me = lax.axis_index(axis)
    sub = lax.slice_in_dim(piece, 0, size, axis=pieces_axis)
    for m in range(1, parts):
        part = lax.slice_in_dim(piece, m * size, (m + 1) * size, axis=pieces_axis)
        got = lax.ppermute(part, axis, [(k, m * owners + k) for k in range(owners)])
        sub = jnp.where(me // owners == m, got, sub)
    return lax.all_gather(sub, axis, axis=0, tiled=False), parts, size


def on_device(front_blocks, child_updates, child_map, row_count, col_count):
    row_index = lax.axis_index("row")
    col_index = lax.axis_index("col")
    slots_r, tile, slots_c, _ = front_blocks.shape
    child_count, kr_count, _, kc_count, _ = child_updates.shape
    home, shift, start, inv = decode_map(child_map, col_count)
    groups = home.shape[1]

    dense = []
    for i in range(child_count):
        with jax.named_scope("child_route"):
            x = child_updates[i].reshape(groups, kr_count // groups, tile, kc_count, tile)
            x = jnp.take(x, inv[i], axis=0)
            x = jnp.take(x, inv[i], axis=3)
            packets = jnp.transpose(x, (0, 3, 1, 2, 4))
            got = routed(packets, start[i], row_count, col_count)
            z = jnp.transpose(got, (0, 2, 3, 1, 4)).reshape(groups * 2, tile, groups, tile)
        with jax.named_scope("child_place"):
            qs = jnp.arange(groups)
            a_of = inv[i]
            s_of = shift[i, a_of]
            h_of = home[i, a_of]
            src = (start[i] + qs - row_index) % row_count
            per_home = col_count // row_count
            first = ((s_of - src) % col_count) // row_count
            row_slot = jnp.stack(
                [per_home * h_of + first, per_home * h_of + 1 - first], axis=1
            ).reshape(-1)
            col_slot = h_of
            row_src = jnp.sum(
                jnp.where(
                    row_slot[None, :] == jnp.arange(slots_r)[:, None],
                    jnp.arange(groups * 2)[None, :] + 1,
                    0,
                ),
                axis=1,
            ) - 1
            row_src = jnp.where(row_src < 0, groups * 2, row_src)
            col_src = jnp.sum(
                jnp.where(
                    col_slot[None, :] == jnp.arange(slots_c)[:, None],
                    jnp.arange(groups)[None, :] + 1,
                    0,
                ),
                axis=1,
            ) - 1
            col_src = jnp.where(col_src < 0, groups, col_src)
            zp = jnp.concatenate([z, jnp.zeros((1, tile, groups, tile), z.dtype)], axis=0)
            zp = jnp.take(zp, row_src, axis=0)
            zp = jnp.concatenate([zp, jnp.zeros((slots_r, tile, 1, tile), z.dtype)], axis=2)
            dense.append(jnp.take(zp, col_src, axis=2))

    with jax.named_scope("assemble"):
        assembled = front_blocks
        for d in dense:
            assembled = assembled + d.astype(jnp.float32)
        height = slots_r * tile
        breadth = slots_c * tile
        a2 = assembled.reshape(height, breadth)

    local_rows = jnp.arange(height, dtype=jnp.int32)
    row_global = (local_rows // tile * row_count + row_index) * tile + local_rows % tile
    local_cols = jnp.arange(breadth, dtype=jnp.int32)
    col_global = (local_cols // tile * col_count + col_index) * tile + local_cols % tile
    owners = PD // tile

    with jax.named_scope("gather_panel_rows"):
        g, parts, size = spread_pieces(a2[:, 0:tile], "col", owners, col_count, 0)
        g = g.reshape(parts, owners, size, tile).transpose(0, 2, 1, 3)
        g_rows = g.reshape(height, PD)
    with jax.named_scope("gather_panel_cols"):
        g, parts, size = spread_pieces(a2[0:tile, :], "row", owners, row_count, 0)
        g = g.reshape(parts, owners, size, breadth).transpose(1, 0, 2, 3)
        g_cols = g.reshape(PD, breadth)
    with jax.named_scope("gather_diagonal"):
        g, parts, size = spread_pieces(g_rows[0:tile, :], "row", owners, row_count, 0)
        g = g.reshape(parts, owners, size, PD).transpose(1, 0, 2, 3)
        diag = g.reshape(PD, PD)

    with jax.named_scope("factor_diagonal"):
        factor = jnp.linalg.cholesky(diag)
        w = lax.linalg.triangular_solve(
            factor, jnp.eye(PD, dtype=jnp.float32), left_side=True, lower=True
        ).T

    def panel_rows(block, gidx):
        solved = jnp.dot(block, w, precision=HI)
        inside = jnp.take(factor, jnp.clip(gidx, 0, PD - 1), axis=0)
        return jnp.where((gidx >= PD)[:, None], solved, inside)

    with jax.named_scope("panel_factors"):
        pr = panel_rows(g_rows, row_global)
        pc = panel_rows(g_cols.T, col_global)

    with jax.named_scope("trailing_update"):
        out = a2 - jnp.dot(pr, pc.T, precision=HI)
        own = lax.dynamic_slice_in_dim(pr, jnp.minimum(col_index, owners - 1) * tile, tile, axis=1)
        first = jnp.where(col_index < owners, own, out[:, 0:tile])
        out = out.at[:, 0:tile].set(first)
        upper = (row_global[:, None] < PD) & (col_global[None, :] >= PD)
        out = jnp.where(upper, 0.0, out)
    return out.reshape(slots_r, tile, slots_c, tile)


def solution(mesh):
    placed = (P(None, "row", None, "col"), P(None, None, "row", None, "col"), P())
    row_count = mesh.shape["row"]
    col_count = mesh.shape["col"]

    def body(front_blocks, child_updates, child_map):
        return on_device(front_blocks, child_updates, child_map, row_count, col_count)

    return jax.shard_map(
        body,
        mesh=mesh,
        in_specs=placed,
        out_specs=P(None, "row", None, "col"),
        check_vma=False,
    )
```

```python
import functools

import jax
import jax.numpy as jnp
from jax import lax
from jax.experimental import pallas as pl
from jax.experimental.pallas import tpu as pltpu
from jax.sharding import PartitionSpec as P

PW = 256
PANELS = 2
PD = 512
HI = lax.Precision.HIGHEST
MESH = pl.DeviceIdType.MESH


def decode_map(child_map, lanes):
    base = child_map[:, ::lanes]
    home = base // lanes
    shift = base % lanes
    groups = base.shape[1]
    prev = (shift - 1) % lanes
    has_prev = jnp.any(prev[:, :, None] == shift[:, None, :], axis=2)
    start = jnp.sum(jnp.where(has_prev, 0, shift), axis=1)
    order = (shift - start[:, None]) % lanes
    picks = order[:, :, None] == jnp.arange(groups)[None, None, :]
    inv = jnp.sum(jnp.where(picks, jnp.arange(groups)[None, :, None], 0), axis=1)
    return home, shift, start, inv


def route_kernel(sigma, groups, row_count, col_count, pk_ref, out_ref, send_sem, recv_sem):
    row_at = lax.axis_index("row")
    col_at = lax.axis_index("col")
    sig_r = sigma % row_count
    targets = []
    for qr in range(groups):
        to_row = lax.rem(sig_r + qr - row_at + row_count, row_count)
        for qc in range(groups):
            to_col = lax.rem(sigma + qc - col_at + col_count, col_count)
            mine = (to_row == row_at) & (to_col == col_at)
            targets.append((qr, qc, to_row, to_col, mine))
    barrier = pltpu.get_barrier_semaphore()
    for qr, qc, to_row, to_col, mine in targets:

        @pl.when(jnp.logical_not(mine))
        def _():
            pl.semaphore_signal(barrier, 1, device_id=(to_row, to_col), device_id_type=MESH)

    peers = sum(jnp.logical_not(t[4]).astype(jnp.int32) for t in targets)
    pl.semaphore_wait(barrier, peers)

    copies = []
    for n, (qr, qc, to_row, to_col, mine) in enumerate(targets):
        remote = pltpu.make_async_remote_copy(
            src_ref=pk_ref.at[qr, qc],
            dst_ref=out_ref.at[qr, qc],
            send_sem=send_sem.at[n],
            recv_sem=recv_sem.at[n],
            device_id=(to_row, to_col),
            device_id_type=MESH,
        )
        local = pltpu.make_async_copy(pk_ref.at[qr, qc], out_ref.at[qr, qc], recv_sem.at[n])
        copies.append((remote, local, mine))

        @pl.when(jnp.logical_not(mine))
        def _():
            remote.start()

        @pl.when(mine)
        def _():
            local.start()

    for remote, local, mine in copies:

        @pl.when(jnp.logical_not(mine))
        def _():
            remote.wait()

        @pl.when(mine)
        def _():
            local.wait()


def route_call(packets, sigma, row_count, col_count):
    groups = packets.shape[0]
    count = groups * groups
    return pl.pallas_call(
        functools.partial(route_kernel, sigma, groups, row_count, col_count),
        out_shape=jax.ShapeDtypeStruct(packets.shape, packets.dtype),
        in_specs=[pl.BlockSpec(memory_space=pl.ANY)],
        out_specs=pl.BlockSpec(memory_space=pl.ANY),
        scratch_shapes=[pltpu.SemaphoreType.DMA((count,)), pltpu.SemaphoreType.DMA((count,))],
        compiler_params=pltpu.CompilerParams(collective_id=sigma, has_side_effects=True),
        name=f"route_{sigma}",
    )(packets)


def routed(packets, start, row_count, col_count):
    branches = [
        functools.partial(route_call, sigma=sg, row_count=row_count, col_count=col_count)
        for sg in range(col_count)
    ]
    return lax.switch(start % col_count, branches, packets)


def spread_pieces(piece, axis, owners, devices, pieces_axis):
    parts = devices // owners
    size = piece.shape[pieces_axis] // parts
    me = lax.axis_index(axis)
    sub = lax.slice_in_dim(piece, 0, size, axis=pieces_axis)
    for m in range(1, parts):
        part = lax.slice_in_dim(piece, m * size, (m + 1) * size, axis=pieces_axis)
        got = lax.ppermute(part, axis, [(k, m * owners + k) for k in range(owners)])
        sub = jnp.where(me // owners == m, got, sub)
    return lax.all_gather(sub, axis, axis=0, tiled=False), parts, size


def on_device(front_blocks, child_updates, child_map, row_count, col_count):
    row_index = lax.axis_index("row")
    col_index = lax.axis_index("col")
    slots_r, tile, slots_c, _ = front_blocks.shape
    child_count, kr_count, _, kc_count, _ = child_updates.shape
    home, shift, start, inv = decode_map(child_map, col_count)
    groups = home.shape[1]

    dense = []
    for i in range(child_count):
        with jax.named_scope("child_route"):
            x = child_updates[i].reshape(groups, kr_count // groups, tile, kc_count, tile)
            x = jnp.take(x, inv[i], axis=0)
            x = jnp.take(x, inv[i], axis=3)
            packets = jnp.transpose(x, (0, 3, 1, 2, 4))
            got = routed(packets, start[i], row_count, col_count)
            z = jnp.transpose(got, (0, 2, 3, 1, 4)).reshape(groups * 2, tile, groups, tile)
        with jax.named_scope("child_place"):
            qs = jnp.arange(groups)
            a_of = inv[i]
            s_of = shift[i, a_of]
            h_of = home[i, a_of]
            src = (start[i] + qs - row_index) % row_count
            per_home = col_count // row_count
            first = ((s_of - src) % col_count) // row_count
            row_slot = jnp.stack(
                [per_home * h_of + first, per_home * h_of + 1 - first], axis=1
            ).reshape(-1)
            col_slot = h_of
            row_src = jnp.sum(
                jnp.where(
                    row_slot[None, :] == jnp.arange(slots_r)[:, None],
                    jnp.arange(groups * 2)[None, :] + 1,
                    0,
                ),
                axis=1,
            ) - 1
            row_src = jnp.where(row_src < 0, groups * 2, row_src)
            col_src = jnp.sum(
                jnp.where(
                    col_slot[None, :] == jnp.arange(slots_c)[:, None],
                    jnp.arange(groups)[None, :] + 1,
                    0,
                ),
                axis=1,
            ) - 1
            col_src = jnp.where(col_src < 0, groups, col_src)
            zp = jnp.concatenate([z, jnp.zeros((1, tile, groups, tile), z.dtype)], axis=0)
            zp = jnp.take(zp, row_src, axis=0)
            zp = jnp.concatenate([zp, jnp.zeros((slots_r, tile, 1, tile), z.dtype)], axis=2)
            dense.append(jnp.take(zp, col_src, axis=2))

    with jax.named_scope("assemble"):
        assembled = front_blocks
        for d in dense:
            assembled = assembled + d.astype(jnp.float32)
        height = slots_r * tile
        breadth = slots_c * tile
        a2 = assembled.reshape(height, breadth)

    local_rows = jnp.arange(height, dtype=jnp.int32)
    row_global = (local_rows // tile * row_count + row_index) * tile + local_rows % tile
    local_cols = jnp.arange(breadth, dtype=jnp.int32)
    col_global = (local_cols // tile * col_count + col_index) * tile + local_cols % tile
    owners = PD // tile

    with jax.named_scope("gather_diagonal"):
        g, parts, size = spread_pieces(a2[0:tile, 0:tile], "col", owners, col_count, 0)
        g = g.reshape(parts, owners, size, tile).transpose(0, 2, 1, 3)
        strip = g.reshape(tile, PD)
        g, parts, size = spread_pieces(strip, "row", owners, row_count, 0)
        g = g.reshape(parts, owners, size, PD).transpose(1, 0, 2, 3)
        diag = g.reshape(PD, PD)
    with jax.named_scope("gather_panel_rows"):
        g, parts, size = spread_pieces(a2[:, 0:tile], "col", owners, col_count, 0)
        g = g.reshape(parts, owners, size, tile).transpose(0, 2, 1, 3)
        g_rows = g.reshape(height, PD)
    with jax.named_scope("gather_panel_cols"):
        g, parts, size = spread_pieces(a2[0:tile, :], "row", owners, row_count, 0)
        g = g.reshape(parts, owners, size, breadth).transpose(1, 0, 2, 3)
        g_cols = g.reshape(PD, breadth)

    with jax.named_scope("factor_diagonal"):
        factor = jnp.linalg.cholesky(diag)
        w = lax.linalg.triangular_solve(
            factor, jnp.eye(PD, dtype=jnp.float32), left_side=True, lower=True
        ).T

    def panel_rows(block, at):
        solved = jnp.dot(block, w, precision=HI)
        inside = lax.dynamic_slice_in_dim(factor, jnp.minimum(at, owners - 1) * tile, tile, axis=0)
        head = jnp.where(at < owners, inside, solved[0:tile])
        return lax.dynamic_update_slice_in_dim(solved, head, 0, axis=0)

    with jax.named_scope("panel_factors"):
        pr = panel_rows(g_rows, row_index)
        pc = panel_rows(g_cols.T, col_index)

    with jax.named_scope("trailing_update"):
        out = a2 - jnp.dot(pr, pc.T, precision=HI)
        own = lax.dynamic_slice_in_dim(pr, jnp.minimum(col_index, owners - 1) * tile, tile, axis=1)
        first = jnp.where(col_index < owners, own, out[:, 0:tile])
        out = lax.dynamic_update_slice_in_dim(out, first, 0, axis=1)
        top = out[0:tile]
        top = jnp.where((row_index < owners) & (col_global >= PD)[None, :], 0.0, top)
        out = lax.dynamic_update_slice_in_dim(out, top, 0, axis=0)
    return out.reshape(slots_r, tile, slots_c, tile)


def solution(mesh):
    placed = (P(None, "row", None, "col"), P(None, None, "row", None, "col"), P())
    row_count = mesh.shape["row"]
    col_count = mesh.shape["col"]

    def body(front_blocks, child_updates, child_map):
        return on_device(front_blocks, child_updates, child_map, row_count, col_count)

    return jax.shard_map(
        body,
        mesh=mesh,
        in_specs=placed,
        out_specs=P(None, "row", None, "col"),
        check_vma=False,
    )
```

```python
import functools

import jax
import jax.numpy as jnp
from jax import lax
from jax.experimental import pallas as pl
from jax.experimental.pallas import tpu as pltpu
from jax.sharding import PartitionSpec as P

PW = 256
PANELS = 2
PD = 512
HI = lax.Precision.HIGHEST
MESH = pl.DeviceIdType.MESH


def decode_map(child_map, lanes):
    base = child_map[:, ::lanes]
    home = base // lanes
    shift = base % lanes
    groups = base.shape[1]
    prev = (shift - 1) % lanes
    has_prev = jnp.any(prev[:, :, None] == shift[:, None, :], axis=2)
    start = jnp.sum(jnp.where(has_prev, 0, shift), axis=1)
    order = (shift - start[:, None]) % lanes
    picks = order[:, :, None] == jnp.arange(groups)[None, None, :]
    inv = jnp.sum(jnp.where(picks, jnp.arange(groups)[None, :, None], 0), axis=1)
    return home, shift, start, inv


def route_kernel(sigma, groups, row_count, col_count, pk_ref, out_ref, send_sem, recv_sem):
    row_at = lax.axis_index("row")
    col_at = lax.axis_index("col")
    sig_r = sigma % row_count
    targets = []
    for qr in range(groups):
        to_row = lax.rem(sig_r + qr - row_at + row_count, row_count)
        for qc in range(groups):
            to_col = lax.rem(sigma + qc - col_at + col_count, col_count)
            mine = (to_row == row_at) & (to_col == col_at)
            targets.append((qr, qc, to_row, to_col, mine))
    barrier = pltpu.get_barrier_semaphore()
    for qr, qc, to_row, to_col, mine in targets:

        @pl.when(jnp.logical_not(mine))
        def _():
            pl.semaphore_signal(barrier, 1, device_id=(to_row, to_col), device_id_type=MESH)

    peers = sum(jnp.logical_not(t[4]).astype(jnp.int32) for t in targets)
    pl.semaphore_wait(barrier, peers)

    copies = []
    for n, (qr, qc, to_row, to_col, mine) in enumerate(targets):
        remote = pltpu.make_async_remote_copy(
            src_ref=pk_ref.at[qr, qc],
            dst_ref=out_ref.at[qr, qc],
            send_sem=send_sem.at[n],
            recv_sem=recv_sem.at[n],
            device_id=(to_row, to_col),
            device_id_type=MESH,
        )
        local = pltpu.make_async_copy(pk_ref.at[qr, qc], out_ref.at[qr, qc], recv_sem.at[n])
        copies.append((remote, local, mine))

        @pl.when(jnp.logical_not(mine))
        def _():
            remote.start()

        @pl.when(mine)
        def _():
            local.start()

    for remote, local, mine in copies:

        @pl.when(jnp.logical_not(mine))
        def _():
            remote.wait()

        @pl.when(mine)
        def _():
            local.wait()


def route_call(packets, sigma, row_count, col_count):
    groups = packets.shape[0]
    count = groups * groups
    return pl.pallas_call(
        functools.partial(route_kernel, sigma, groups, row_count, col_count),
        out_shape=jax.ShapeDtypeStruct(packets.shape, packets.dtype),
        in_specs=[pl.BlockSpec(memory_space=pl.ANY)],
        out_specs=pl.BlockSpec(memory_space=pl.ANY),
        scratch_shapes=[pltpu.SemaphoreType.DMA((count,)), pltpu.SemaphoreType.DMA((count,))],
        compiler_params=pltpu.CompilerParams(collective_id=sigma, has_side_effects=True),
        name=f"route_{sigma}",
    )(packets)


def routed(packets, start, row_count, col_count):
    branches = [
        functools.partial(route_call, sigma=sg, row_count=row_count, col_count=col_count)
        for sg in range(col_count)
    ]
    return lax.switch(start % col_count, branches, packets)


def spread_pieces(piece, axis, owners, devices, pieces_axis):
    parts = devices // owners
    size = piece.shape[pieces_axis] // parts
    me = lax.axis_index(axis)
    sub = lax.slice_in_dim(piece, 0, size, axis=pieces_axis)
    for m in range(1, parts):
        part = lax.slice_in_dim(piece, m * size, (m + 1) * size, axis=pieces_axis)
        got = lax.ppermute(part, axis, [(k, m * owners + k) for k in range(owners)])
        sub = jnp.where(me // owners == m, got, sub)
    return lax.all_gather(sub, axis, axis=0, tiled=False), parts, size


def on_device(front_blocks, child_updates, child_map, row_count, col_count):
    row_index = lax.axis_index("row")
    col_index = lax.axis_index("col")
    slots_r, tile, slots_c, _ = front_blocks.shape
    child_count, kr_count, _, kc_count, _ = child_updates.shape
    home, shift, start, inv = decode_map(child_map, col_count)
    groups = home.shape[1]

    dense = []
    for i in range(child_count):
        with jax.named_scope("child_route"):
            x = child_updates[i].reshape(groups, kr_count // groups, tile, kc_count, tile)
            x = jnp.take(x, inv[i], axis=0)
            x = jnp.take(x, inv[i], axis=3)
            packets = jnp.transpose(x, (0, 3, 1, 2, 4))
            got = routed(packets, start[i], row_count, col_count)
            z = jnp.transpose(got, (0, 2, 3, 1, 4)).reshape(groups * 2, tile, groups, tile)
        with jax.named_scope("child_place"):
            qs = jnp.arange(groups)
            a_of = inv[i]
            s_of = shift[i, a_of]
            h_of = home[i, a_of]
            src = (start[i] + qs - row_index) % row_count
            per_home = col_count // row_count
            first = ((s_of - src) % col_count) // row_count
            row_slot = jnp.stack(
                [per_home * h_of + first, per_home * h_of + 1 - first], axis=1
            ).reshape(-1)
            col_slot = h_of
            row_src = jnp.sum(
                jnp.where(
                    row_slot[None, :] == jnp.arange(slots_r)[:, None],
                    jnp.arange(groups * 2)[None, :] + 1,
                    0,
                ),
                axis=1,
            ) - 1
            row_src = jnp.where(row_src < 0, groups * 2, row_src)
            col_src = jnp.sum(
                jnp.where(
                    col_slot[None, :] == jnp.arange(slots_c)[:, None],
                    jnp.arange(groups)[None, :] + 1,
                    0,
                ),
                axis=1,
            ) - 1
            col_src = jnp.where(col_src < 0, groups, col_src)
            zp = jnp.concatenate([z, jnp.zeros((1, tile, groups, tile), z.dtype)], axis=0)
            zp = jnp.take(zp, row_src, axis=0)
            zp = jnp.concatenate([zp, jnp.zeros((slots_r, tile, 1, tile), z.dtype)], axis=2)
            dense.append(jnp.take(zp, col_src, axis=2))

    with jax.named_scope("assemble"):
        assembled = front_blocks
        for d in dense:
            assembled = assembled + d.astype(jnp.float32)
        height = slots_r * tile
        breadth = slots_c * tile
        a2 = assembled.reshape(height, breadth)

    local_rows = jnp.arange(height, dtype=jnp.int32)
    row_global = (local_rows // tile * row_count + row_index) * tile + local_rows % tile
    local_cols = jnp.arange(breadth, dtype=jnp.int32)
    col_global = (local_cols // tile * col_count + col_index) * tile + local_cols % tile
    owners = PD // tile

    with jax.named_scope("gather_diagonal"):
        g, parts, size = spread_pieces(a2[0:tile, 0:tile], "col", owners, col_count, 0)
        g = g.reshape(parts, owners, size, tile).transpose(0, 2, 1, 3)
        strip = g.reshape(tile, PD)
        g, parts, size = spread_pieces(strip, "row", owners, row_count, 0)
        g = g.reshape(parts, owners, size, PD).transpose(1, 0, 2, 3)
        diag = g.reshape(PD, PD)
    with jax.named_scope("gather_panel_rows"):
        g, parts, size = spread_pieces(a2[:, 0:tile], "col", owners, col_count, 0)
        g = g.reshape(parts, owners, size, tile).transpose(0, 2, 1, 3)
        g_rows = g.reshape(height, PD)
    with jax.named_scope("gather_panel_cols"):
        g, parts, size = spread_pieces(a2[0:tile, :], "row", owners, row_count, 0)
        g = g.reshape(parts, owners, size, breadth).transpose(1, 0, 2, 3)
        g_cols = g.reshape(PD, breadth)

    with jax.named_scope("factor_diagonal"):
        factor, w = blocked_factor(diag, tile)

    def panel_rows(block, at):
        solved = jnp.dot(block, w, precision=lax.Precision.HIGH)
        inside = lax.dynamic_slice_in_dim(factor, jnp.minimum(at, owners - 1) * tile, tile, axis=0)
        head = jnp.where(at < owners, inside, solved[0:tile])
        return lax.dynamic_update_slice_in_dim(solved, head, 0, axis=0)

    with jax.named_scope("panel_factors"):
        pr = panel_rows(g_rows, row_index)
        pc = panel_rows(g_cols.T, col_index)

    with jax.named_scope("trailing_update"):
        out = a2 - jnp.dot(pr, pc.T, precision=lax.Precision.HIGH)
        own = lax.dynamic_slice_in_dim(pr, jnp.minimum(col_index, owners - 1) * tile, tile, axis=1)
        first = jnp.where(col_index < owners, own, out[:, 0:tile])
        out = lax.dynamic_update_slice_in_dim(out, first, 0, axis=1)
        top = out[0:tile]
        top = jnp.where((row_index < owners) & (col_global >= PD)[None, :], 0.0, top)
        out = lax.dynamic_update_slice_in_dim(out, top, 0, axis=0)
    return out.reshape(slots_r, tile, slots_c, tile)


def blocked_factor(matrix, size):
    count = matrix.shape[0] // size
    eye = jnp.eye(size, dtype=matrix.dtype)
    matrix = 0.5 * (matrix + matrix.T)
    blocks = [[matrix[i * size : (i + 1) * size, k * size : (k + 1) * size] for k in range(count)] for i in range(count)]
    low = [[None] * count for _ in range(count)]
    inv = [[None] * count for _ in range(count)]
    for k in range(count):
        low[k][k] = lax.linalg.cholesky(blocks[k][k], symmetrize_input=False)
        inv[k][k] = lax.linalg.triangular_solve(low[k][k], eye, left_side=True, lower=True)
        if k + 1 < count:
            below = jnp.concatenate([blocks[i][k] for i in range(k + 1, count)], axis=0)
            solved = jnp.dot(below, inv[k][k].T, precision=HI)
            for n, i in enumerate(range(k + 1, count)):
                low[i][k] = solved[n * size : (n + 1) * size]
            rest = jnp.dot(solved, solved.T, precision=HI)
            for n, i in enumerate(range(k + 1, count)):
                for m, j in enumerate(range(k + 1, count)):
                    blocks[i][j] = blocks[i][j] - rest[n * size : (n + 1) * size, m * size : (m + 1) * size]
    for j in range(count):
        for i in range(j + 1, count):
            acc = sum(jnp.dot(low[i][k], inv[k][j], precision=HI) for k in range(j, i))
            inv[i][j] = -jnp.dot(inv[i][i], acc, precision=HI)
    zero = jnp.zeros((size, size), matrix.dtype)
    factor = jnp.concatenate(
        [jnp.concatenate([low[i][k] if k <= i else zero for k in range(count)], axis=1) for i in range(count)], axis=0
    )
    inverse = jnp.concatenate(
        [jnp.concatenate([inv[i][k] if k <= i else zero for k in range(count)], axis=1) for i in range(count)], axis=0
    )
    return factor, inverse.T


def solution(mesh):
    placed = (P(None, "row", None, "col"), P(None, None, "row", None, "col"), P())
    row_count = mesh.shape["row"]
    col_count = mesh.shape["col"]

    def body(front_blocks, child_updates, child_map):
        return on_device(front_blocks, child_updates, child_map, row_count, col_count)

    return jax.shard_map(
        body,
        mesh=mesh,
        in_specs=placed,
        out_specs=P(None, "row", None, "col"),
        check_vma=False,
    )
```

```python
import functools

import jax
import jax.numpy as jnp
from jax import lax
from jax.experimental import pallas as pl
from jax.experimental.pallas import tpu as pltpu
from jax.sharding import PartitionSpec as P

PW = 256
PANELS = 2
PD = 512
HI = lax.Precision.HIGHEST
MESH = pl.DeviceIdType.MESH


def decode_map(child_map, lanes):
    base = child_map[:, ::lanes]
    home = base // lanes
    shift = base % lanes
    groups = base.shape[1]
    prev = (shift - 1) % lanes
    has_prev = jnp.any(prev[:, :, None] == shift[:, None, :], axis=2)
    start = jnp.sum(jnp.where(has_prev, 0, shift), axis=1)
    order = (shift - start[:, None]) % lanes
    picks = order[:, :, None] == jnp.arange(groups)[None, None, :]
    inv = jnp.sum(jnp.where(picks, jnp.arange(groups)[None, :, None], 0), axis=1)
    return home, shift, start, inv


def route_kernel(sigma, groups, row_count, col_count, pk_ref, out_ref, send_sem, recv_sem):
    row_at = lax.axis_index("row")
    col_at = lax.axis_index("col")
    sig_r = sigma % row_count
    targets = []
    for qr in range(groups):
        to_row = lax.rem(sig_r + qr - row_at + row_count, row_count)
        for qc in range(groups):
            to_col = lax.rem(sigma + qc - col_at + col_count, col_count)
            mine = (to_row == row_at) & (to_col == col_at)
            targets.append((qr, qc, to_row, to_col, mine))
    barrier = pltpu.get_barrier_semaphore()
    for qr, qc, to_row, to_col, mine in targets:

        @pl.when(jnp.logical_not(mine))
        def _():
            pl.semaphore_signal(barrier, 1, device_id=(to_row, to_col), device_id_type=MESH)

    peers = sum(jnp.logical_not(t[4]).astype(jnp.int32) for t in targets)
    pl.semaphore_wait(barrier, peers)

    copies = []
    for n, (qr, qc, to_row, to_col, mine) in enumerate(targets):
        remote = pltpu.make_async_remote_copy(
            src_ref=pk_ref.at[qr, qc],
            dst_ref=out_ref.at[qr, qc],
            send_sem=send_sem.at[n],
            recv_sem=recv_sem.at[n],
            device_id=(to_row, to_col),
            device_id_type=MESH,
        )
        local = pltpu.make_async_copy(pk_ref.at[qr, qc], out_ref.at[qr, qc], recv_sem.at[n])
        copies.append((remote, local, mine))

        @pl.when(jnp.logical_not(mine))
        def _():
            remote.start()

        @pl.when(mine)
        def _():
            local.start()

    for remote, local, mine in copies:

        @pl.when(jnp.logical_not(mine))
        def _():
            remote.wait()

        @pl.when(mine)
        def _():
            local.wait()


def route_call(packets, sigma, row_count, col_count):
    groups = packets.shape[0]
    count = groups * groups
    return pl.pallas_call(
        functools.partial(route_kernel, sigma, groups, row_count, col_count),
        out_shape=jax.ShapeDtypeStruct(packets.shape, packets.dtype),
        in_specs=[pl.BlockSpec(memory_space=pl.ANY)],
        out_specs=pl.BlockSpec(memory_space=pl.ANY),
        scratch_shapes=[pltpu.SemaphoreType.DMA((count,)), pltpu.SemaphoreType.DMA((count,))],
        compiler_params=pltpu.CompilerParams(collective_id=sigma, has_side_effects=True),
        name=f"route_{sigma}",
    )(packets)


def routed(packets, start, row_count, col_count):
    branches = [
        functools.partial(route_call, sigma=sg, row_count=row_count, col_count=col_count)
        for sg in range(col_count)
    ]
    return lax.switch(start % col_count, branches, packets)


def spread_pieces(piece, axis, owners, devices, pieces_axis):
    parts = devices // owners
    size = piece.shape[pieces_axis] // parts
    me = lax.axis_index(axis)
    sub = lax.slice_in_dim(piece, 0, size, axis=pieces_axis)
    for m in range(1, parts):
        part = lax.slice_in_dim(piece, m * size, (m + 1) * size, axis=pieces_axis)
        got = lax.ppermute(part, axis, [(k, m * owners + k) for k in range(owners)])
        sub = jnp.where(me // owners == m, got, sub)
    return lax.all_gather(sub, axis, axis=0, tiled=False), parts, size


def on_device(front_blocks, child_updates, child_map, row_count, col_count):
    row_index = lax.axis_index("row")
    col_index = lax.axis_index("col")
    slots_r, tile, slots_c, _ = front_blocks.shape
    child_count, kr_count, _, kc_count, _ = child_updates.shape
    home, shift, start, inv = decode_map(child_map, col_count)
    groups = home.shape[1]

    dense = []
    for i in range(child_count):
        with jax.named_scope("child_route"):
            x = child_updates[i].reshape(groups, kr_count // groups, tile, kc_count, tile)
            x = jnp.take(x, inv[i], axis=0)
            x = jnp.take(x, inv[i], axis=3)
            packets = jnp.transpose(x, (0, 3, 1, 2, 4))
            got = routed(packets, start[i], row_count, col_count)
            z = jnp.transpose(got, (0, 2, 3, 1, 4)).reshape(groups * 2, tile, groups, tile)
        with jax.named_scope("child_place"):
            qs = jnp.arange(groups)
            a_of = inv[i]
            s_of = shift[i, a_of]
            h_of = home[i, a_of]
            src = (start[i] + qs - row_index) % row_count
            per_home = col_count // row_count
            first = ((s_of - src) % col_count) // row_count
            row_slot = jnp.stack(
                [per_home * h_of + first, per_home * h_of + 1 - first], axis=1
            ).reshape(-1)
            col_slot = h_of
            row_src = jnp.sum(
                jnp.where(
                    row_slot[None, :] == jnp.arange(slots_r)[:, None],
                    jnp.arange(groups * 2)[None, :] + 1,
                    0,
                ),
                axis=1,
            ) - 1
            row_src = jnp.where(row_src < 0, groups * 2, row_src)
            col_src = jnp.sum(
                jnp.where(
                    col_slot[None, :] == jnp.arange(slots_c)[:, None],
                    jnp.arange(groups)[None, :] + 1,
                    0,
                ),
                axis=1,
            ) - 1
            col_src = jnp.where(col_src < 0, groups, col_src)
            zp = jnp.concatenate([z, jnp.zeros((1, tile, groups, tile), z.dtype)], axis=0)
            zp = jnp.take(zp, row_src, axis=0)
            zp = jnp.concatenate([zp, jnp.zeros((slots_r, tile, 1, tile), z.dtype)], axis=2)
            dense.append(jnp.take(zp, col_src, axis=2))

    with jax.named_scope("assemble"):
        assembled = front_blocks
        for d in dense:
            assembled = assembled + d.astype(jnp.float32)
        height = slots_r * tile
        breadth = slots_c * tile
        a2 = assembled.reshape(height, breadth)

    local_rows = jnp.arange(height, dtype=jnp.int32)
    row_global = (local_rows // tile * row_count + row_index) * tile + local_rows % tile
    local_cols = jnp.arange(breadth, dtype=jnp.int32)
    col_global = (local_cols // tile * col_count + col_index) * tile + local_cols % tile
    owners = PD // tile

    with jax.named_scope("gather_diagonal"):
        g = lax.all_gather(a2[0:tile, 0:tile], "col", axis=0, tiled=False)[0:owners]
        strip = jnp.transpose(g, (1, 0, 2)).reshape(tile, PD)
        g = lax.all_gather(strip, "row", axis=0, tiled=False)[0:owners]
        diag = g.reshape(PD, PD)
    with jax.named_scope("gather_panel_rows"):
        g, parts, size = spread_pieces(a2[:, 0:tile], "col", owners, col_count, 0)
        g = g.reshape(parts, owners, size, tile).transpose(0, 2, 1, 3)
        g_rows = g.reshape(height, PD)
    with jax.named_scope("gather_panel_cols"):
        g, parts, size = spread_pieces(a2[0:tile, :], "row", owners, row_count, 0)
        g = g.reshape(parts, owners, size, breadth).transpose(1, 0, 2, 3)
        g_cols = g.reshape(PD, breadth)

    with jax.named_scope("factor_diagonal"):
        factor, w = blocked_factor(diag, tile)

    def panel_rows(block, at):
        solved = jnp.dot(block, w, precision=lax.Precision.HIGH)
        inside = lax.dynamic_slice_in_dim(factor, jnp.minimum(at, owners - 1) * tile, tile, axis=0)
        head = jnp.where(at < owners, inside, solved[0:tile])
        return lax.dynamic_update_slice_in_dim(solved, head, 0, axis=0)

    with jax.named_scope("panel_factors"):
        pr = panel_rows(g_rows, row_index)
        pc = panel_rows(g_cols.T, col_index)

    with jax.named_scope("trailing_update"):
        out = a2 - jnp.dot(pr, pc.T, precision=lax.Precision.HIGH)
        own = lax.dynamic_slice_in_dim(pr, jnp.minimum(col_index, owners - 1) * tile, tile, axis=1)
        first = jnp.where(col_index < owners, own, out[:, 0:tile])
        out = lax.dynamic_update_slice_in_dim(out, first, 0, axis=1)
        top = out[0:tile]
        top = jnp.where((row_index < owners) & (col_global >= PD)[None, :], 0.0, top)
        out = lax.dynamic_update_slice_in_dim(out, top, 0, axis=0)
    return out.reshape(slots_r, tile, slots_c, tile)


def blocked_factor(matrix, size):
    count = matrix.shape[0] // size
    eye = jnp.eye(size, dtype=matrix.dtype)
    matrix = 0.5 * (matrix + matrix.T)
    blocks = [[matrix[i * size : (i + 1) * size, k * size : (k + 1) * size] for k in range(count)] for i in range(count)]
    low = [[None] * count for _ in range(count)]
    inv = [[None] * count for _ in range(count)]
    for k in range(count):
        low[k][k] = lax.linalg.cholesky(blocks[k][k], symmetrize_input=False)
        inv[k][k] = lax.linalg.triangular_solve(low[k][k], eye, left_side=True, lower=True)
        if k + 1 < count:
            below = jnp.concatenate([blocks[i][k] for i in range(k + 1, count)], axis=0)
            solved = jnp.dot(below, inv[k][k].T, precision=HI)
            for n, i in enumerate(range(k + 1, count)):
                low[i][k] = solved[n * size : (n + 1) * size]
            rest = jnp.dot(solved, solved.T, precision=HI)
            for n, i in enumerate(range(k + 1, count)):
                for m, j in enumerate(range(k + 1, count)):
                    blocks[i][j] = blocks[i][j] - rest[n * size : (n + 1) * size, m * size : (m + 1) * size]
    for j in range(count):
        for i in range(j + 1, count):
            acc = sum(jnp.dot(low[i][k], inv[k][j], precision=HI) for k in range(j, i))
            inv[i][j] = -jnp.dot(inv[i][i], acc, precision=HI)
    zero = jnp.zeros((size, size), matrix.dtype)
    factor = jnp.concatenate(
        [jnp.concatenate([low[i][k] if k <= i else zero for k in range(count)], axis=1) for i in range(count)], axis=0
    )
    inverse = jnp.concatenate(
        [jnp.concatenate([inv[i][k] if k <= i else zero for k in range(count)], axis=1) for i in range(count)], axis=0
    )
    return factor, inverse.T


def solution(mesh):
    placed = (P(None, "row", None, "col"), P(None, None, "row", None, "col"), P())
    row_count = mesh.shape["row"]
    col_count = mesh.shape["col"]

    def body(front_blocks, child_updates, child_map):
        return on_device(front_blocks, child_updates, child_map, row_count, col_count)

    return jax.shard_map(
        body,
        mesh=mesh,
        in_specs=placed,
        out_specs=P(None, "row", None, "col"),
        check_vma=False,
    )
```

```python
import functools

import jax
import jax.numpy as jnp
from jax import lax
from jax.experimental import pallas as pl
from jax.experimental.pallas import tpu as pltpu
from jax.sharding import PartitionSpec as P

PW = 256
PANELS = 2
PD = 512
HI = lax.Precision.HIGHEST
MESH = pl.DeviceIdType.MESH


def decode_map(child_map, lanes):
    base = child_map[:, ::lanes]
    home = base // lanes
    shift = base % lanes
    groups = base.shape[1]
    prev = (shift - 1) % lanes
    has_prev = jnp.any(prev[:, :, None] == shift[:, None, :], axis=2)
    start = jnp.sum(jnp.where(has_prev, 0, shift), axis=1)
    order = (shift - start[:, None]) % lanes
    picks = order[:, :, None] == jnp.arange(groups)[None, None, :]
    inv = jnp.sum(jnp.where(picks, jnp.arange(groups)[None, :, None], 0), axis=1)
    return home, shift, start, inv


def route_kernel(sigma, groups, row_count, col_count, pk_ref, out_ref, send_sem, recv_sem):
    row_at = lax.axis_index("row")
    col_at = lax.axis_index("col")
    sig_r = sigma % row_count
    targets = []
    for qr in range(groups):
        to_row = lax.rem(sig_r + qr - row_at + row_count, row_count)
        for qc in range(groups):
            to_col = lax.rem(sigma + qc - col_at + col_count, col_count)
            mine = (to_row == row_at) & (to_col == col_at)
            targets.append((qr, qc, to_row, to_col, mine))
    barrier = pltpu.get_barrier_semaphore()
    for qr, qc, to_row, to_col, mine in targets:

        @pl.when(jnp.logical_not(mine))
        def _():
            pl.semaphore_signal(barrier, 1, device_id=(to_row, to_col), device_id_type=MESH)

    peers = sum(jnp.logical_not(t[4]).astype(jnp.int32) for t in targets)
    pl.semaphore_wait(barrier, peers)

    copies = []
    for n, (qr, qc, to_row, to_col, mine) in enumerate(targets):
        remote = pltpu.make_async_remote_copy(
            src_ref=pk_ref.at[qr, qc],
            dst_ref=out_ref.at[qr, qc],
            send_sem=send_sem.at[n],
            recv_sem=recv_sem.at[n],
            device_id=(to_row, to_col),
            device_id_type=MESH,
        )
        local = pltpu.make_async_copy(pk_ref.at[qr, qc], out_ref.at[qr, qc], recv_sem.at[n])
        copies.append((remote, local, mine))

        @pl.when(jnp.logical_not(mine))
        def _():
            remote.start()

        @pl.when(mine)
        def _():
            local.start()

    for remote, local, mine in copies:

        @pl.when(jnp.logical_not(mine))
        def _():
            remote.wait()

        @pl.when(mine)
        def _():
            local.wait()


def route_call(packets, sigma, row_count, col_count):
    groups = packets.shape[0]
    count = groups * groups
    return pl.pallas_call(
        functools.partial(route_kernel, sigma, groups, row_count, col_count),
        out_shape=jax.ShapeDtypeStruct(packets.shape, packets.dtype),
        in_specs=[pl.BlockSpec(memory_space=pl.ANY)],
        out_specs=pl.BlockSpec(memory_space=pl.ANY),
        scratch_shapes=[pltpu.SemaphoreType.DMA((count,)), pltpu.SemaphoreType.DMA((count,))],
        compiler_params=pltpu.CompilerParams(collective_id=sigma, has_side_effects=True),
        name=f"route_{sigma}",
    )(packets)


def routed(packets, start, row_count, col_count):
    branches = [
        functools.partial(route_call, sigma=sg, row_count=row_count, col_count=col_count)
        for sg in range(col_count)
    ]
    return lax.switch(start % col_count, branches, packets)


def spread_pieces(piece, axis, owners, devices, pieces_axis):
    parts = devices // owners
    size = piece.shape[pieces_axis] // parts
    me = lax.axis_index(axis)
    sub = lax.slice_in_dim(piece, 0, size, axis=pieces_axis)
    for m in range(1, parts):
        part = lax.slice_in_dim(piece, m * size, (m + 1) * size, axis=pieces_axis)
        got = lax.ppermute(part, axis, [(k, m * owners + k) for k in range(owners)])
        sub = jnp.where(me // owners == m, got, sub)
    return lax.all_gather(sub, axis, axis=0, tiled=False), parts, size


def on_device(front_blocks, child_updates, child_map, row_count, col_count):
    row_index = lax.axis_index("row")
    col_index = lax.axis_index("col")
    slots_r, tile, slots_c, _ = front_blocks.shape
    child_count, kr_count, _, kc_count, _ = child_updates.shape
    home, shift, start, inv = decode_map(child_map, col_count)
    groups = home.shape[1]

    dense = []
    for i in range(child_count):
        with jax.named_scope("child_route"):
            x = child_updates[i].reshape(groups, kr_count // groups, tile, kc_count, tile)
            x = jnp.take(x, inv[i], axis=0)
            x = jnp.take(x, inv[i], axis=3)
            packets = jnp.transpose(x, (0, 3, 1, 2, 4))
            got = routed(packets, start[i], row_count, col_count)
            z = jnp.transpose(got, (0, 2, 3, 1, 4)).reshape(groups * 2, tile, groups, tile)
        with jax.named_scope("child_place"):
            qs = jnp.arange(groups)
            a_of = inv[i]
            s_of = shift[i, a_of]
            h_of = home[i, a_of]
            src = (start[i] + qs - row_index) % row_count
            per_home = col_count // row_count
            first = ((s_of - src) % col_count) // row_count
            row_slot = jnp.stack(
                [per_home * h_of + first, per_home * h_of + 1 - first], axis=1
            ).reshape(-1)
            col_slot = h_of
            row_src = jnp.sum(
                jnp.where(
                    row_slot[None, :] == jnp.arange(slots_r)[:, None],
                    jnp.arange(groups * 2)[None, :] + 1,
                    0,
                ),
                axis=1,
            ) - 1
            row_src = jnp.where(row_src < 0, groups * 2, row_src)
            col_src = jnp.sum(
                jnp.where(
                    col_slot[None, :] == jnp.arange(slots_c)[:, None],
                    jnp.arange(groups)[None, :] + 1,
                    0,
                ),
                axis=1,
            ) - 1
            col_src = jnp.where(col_src < 0, groups, col_src)
            zp = jnp.concatenate([z, jnp.zeros((1, tile, groups, tile), z.dtype)], axis=0)
            zp = jnp.take(zp, row_src, axis=0)
            zp = jnp.concatenate([zp, jnp.zeros((slots_r, tile, 1, tile), z.dtype)], axis=2)
            dense.append(jnp.take(zp, col_src, axis=2))

    with jax.named_scope("assemble"):
        assembled = front_blocks
        for d in dense:
            assembled = assembled + d.astype(jnp.float32)
        height = slots_r * tile
        breadth = slots_c * tile
        a2 = assembled.reshape(height, breadth)

    local_rows = jnp.arange(height, dtype=jnp.int32)
    row_global = (local_rows // tile * row_count + row_index) * tile + local_rows % tile
    local_cols = jnp.arange(breadth, dtype=jnp.int32)
    col_global = (local_cols // tile * col_count + col_index) * tile + local_cols % tile
    owners = PD // tile

    with jax.named_scope("gather_diagonal"):
        g, parts, size = spread_pieces(a2[0:tile, 0:tile], "col", owners, col_count, 0)
        g = g.reshape(parts, owners, size, tile).transpose(0, 2, 1, 3)
        strip = g.reshape(tile, PD)
        g, parts, size = spread_pieces(strip, "row", owners, row_count, 0)
        g = g.reshape(parts, owners, size, PD).transpose(1, 0, 2, 3)
        diag = g.reshape(PD, PD)
    rows_piece, cols_piece, diag = lax.optimization_barrier((a2[:, 0:tile], a2[0:tile, :], diag))
    with jax.named_scope("gather_panel_rows"):
        g, parts, size = spread_pieces(rows_piece, "col", owners, col_count, 0)
        g = g.reshape(parts, owners, size, tile).transpose(0, 2, 1, 3)
        g_rows = g.reshape(height, PD)
    with jax.named_scope("gather_panel_cols"):
        g, parts, size = spread_pieces(cols_piece, "row", owners, row_count, 0)
        g = g.reshape(parts, owners, size, breadth).transpose(1, 0, 2, 3)
        g_cols = g.reshape(PD, breadth)

    with jax.named_scope("factor_diagonal"):
        factor, w = blocked_factor(diag, tile)

    def panel_rows(block, at):
        solved = jnp.dot(block, w, precision=lax.Precision.HIGH)
        inside = lax.dynamic_slice_in_dim(factor, jnp.minimum(at, owners - 1) * tile, tile, axis=0)
        head = jnp.where(at < owners, inside, solved[0:tile])
        return lax.dynamic_update_slice_in_dim(solved, head, 0, axis=0)

    with jax.named_scope("panel_factors"):
        pr = panel_rows(g_rows, row_index)
        pc = panel_rows(g_cols.T, col_index)

    with jax.named_scope("trailing_update"):
        out = a2 - jnp.dot(pr, pc.T, precision=lax.Precision.HIGH)
        own = lax.dynamic_slice_in_dim(pr, jnp.minimum(col_index, owners - 1) * tile, tile, axis=1)
        first = jnp.where(col_index < owners, own, out[:, 0:tile])
        out = lax.dynamic_update_slice_in_dim(out, first, 0, axis=1)
        top = out[0:tile]
        top = jnp.where((row_index < owners) & (col_global >= PD)[None, :], 0.0, top)
        out = lax.dynamic_update_slice_in_dim(out, top, 0, axis=0)
    return out.reshape(slots_r, tile, slots_c, tile)


def blocked_factor(matrix, size):
    count = matrix.shape[0] // size
    eye = jnp.eye(size, dtype=matrix.dtype)
    matrix = 0.5 * (matrix + matrix.T)
    blocks = [[matrix[i * size : (i + 1) * size, k * size : (k + 1) * size] for k in range(count)] for i in range(count)]
    low = [[None] * count for _ in range(count)]
    inv = [[None] * count for _ in range(count)]
    for k in range(count):
        low[k][k] = lax.linalg.cholesky(blocks[k][k], symmetrize_input=False)
        inv[k][k] = lax.linalg.triangular_solve(low[k][k], eye, left_side=True, lower=True)
        if k + 1 < count:
            below = jnp.concatenate([blocks[i][k] for i in range(k + 1, count)], axis=0)
            solved = jnp.dot(below, inv[k][k].T, precision=HI)
            for n, i in enumerate(range(k + 1, count)):
                low[i][k] = solved[n * size : (n + 1) * size]
            rest = jnp.dot(solved, solved.T, precision=HI)
            for n, i in enumerate(range(k + 1, count)):
                for m, j in enumerate(range(k + 1, count)):
                    blocks[i][j] = blocks[i][j] - rest[n * size : (n + 1) * size, m * size : (m + 1) * size]
    for j in range(count):
        for i in range(j + 1, count):
            acc = sum(jnp.dot(low[i][k], inv[k][j], precision=HI) for k in range(j, i))
            inv[i][j] = -jnp.dot(inv[i][i], acc, precision=HI)
    zero = jnp.zeros((size, size), matrix.dtype)
    factor = jnp.concatenate(
        [jnp.concatenate([low[i][k] if k <= i else zero for k in range(count)], axis=1) for i in range(count)], axis=0
    )
    inverse = jnp.concatenate(
        [jnp.concatenate([inv[i][k] if k <= i else zero for k in range(count)], axis=1) for i in range(count)], axis=0
    )
    return factor, inverse.T


def solution(mesh):
    placed = (P(None, "row", None, "col"), P(None, None, "row", None, "col"), P())
    row_count = mesh.shape["row"]
    col_count = mesh.shape["col"]

    def body(front_blocks, child_updates, child_map):
        return on_device(front_blocks, child_updates, child_map, row_count, col_count)

    return jax.shard_map(
        body,
        mesh=mesh,
        in_specs=placed,
        out_specs=P(None, "row", None, "col"),
        check_vma=False,
    )
```

```python
import functools

import jax
import jax.numpy as jnp
from jax import lax
from jax.experimental import pallas as pl
from jax.experimental.pallas import tpu as pltpu
from jax.sharding import PartitionSpec as P

PW = 256
PANELS = 2
PD = 512
HI = lax.Precision.HIGHEST
MESH = pl.DeviceIdType.MESH


def decode_map(child_map, lanes):
    base = child_map[:, ::lanes]
    home = base // lanes
    shift = base % lanes
    groups = base.shape[1]
    prev = (shift - 1) % lanes
    has_prev = jnp.any(prev[:, :, None] == shift[:, None, :], axis=2)
    start = jnp.sum(jnp.where(has_prev, 0, shift), axis=1)
    order = (shift - start[:, None]) % lanes
    picks = order[:, :, None] == jnp.arange(groups)[None, None, :]
    inv = jnp.sum(jnp.where(picks, jnp.arange(groups)[None, :, None], 0), axis=1)
    return home, shift, start, inv


def route_kernel(sigma, groups, row_count, col_count, pk_ref, out_ref, send_sem, recv_sem):
    row_at = lax.axis_index("row")
    col_at = lax.axis_index("col")
    sig_r = sigma % row_count
    targets = []
    for n in range(groups * groups):
        qr = n % groups
        qc = (n % groups + n // groups) % groups
        to_row = lax.rem(sig_r + qr - row_at + row_count, row_count)
        to_col = lax.rem(sigma + qc - col_at + col_count, col_count)
        mine = (to_row == row_at) & (to_col == col_at)
        targets.append((qr, qc, to_row, to_col, mine))
    barrier = pltpu.get_barrier_semaphore()
    for qr, qc, to_row, to_col, mine in targets:

        @pl.when(jnp.logical_not(mine))
        def _():
            pl.semaphore_signal(barrier, 1, device_id=(to_row, to_col), device_id_type=MESH)

    peers = sum(jnp.logical_not(t[4]).astype(jnp.int32) for t in targets)
    pl.semaphore_wait(barrier, peers)

    copies = []
    for n, (qr, qc, to_row, to_col, mine) in enumerate(targets):
        remote = pltpu.make_async_remote_copy(
            src_ref=pk_ref.at[qr, qc],
            dst_ref=out_ref.at[qr, qc],
            send_sem=send_sem.at[n],
            recv_sem=recv_sem.at[n],
            device_id=(to_row, to_col),
            device_id_type=MESH,
        )
        local = pltpu.make_async_copy(pk_ref.at[qr, qc], out_ref.at[qr, qc], recv_sem.at[n])
        copies.append((remote, local, mine))

        @pl.when(jnp.logical_not(mine))
        def _():
            remote.start()

        @pl.when(mine)
        def _():
            local.start()

    for remote, local, mine in copies:

        @pl.when(jnp.logical_not(mine))
        def _():
            remote.wait()

        @pl.when(mine)
        def _():
            local.wait()


def route_call(packets, sigma, row_count, col_count):
    groups = packets.shape[0]
    count = groups * groups
    return pl.pallas_call(
        functools.partial(route_kernel, sigma, groups, row_count, col_count),
        out_shape=jax.ShapeDtypeStruct(packets.shape, packets.dtype),
        in_specs=[pl.BlockSpec(memory_space=pl.ANY)],
        out_specs=pl.BlockSpec(memory_space=pl.ANY),
        scratch_shapes=[pltpu.SemaphoreType.DMA((count,)), pltpu.SemaphoreType.DMA((count,))],
        compiler_params=pltpu.CompilerParams(collective_id=sigma, has_side_effects=True),
        name=f"route_{sigma}",
    )(packets)


def routed(packets, start, row_count, col_count):
    branches = [
        functools.partial(route_call, sigma=sg, row_count=row_count, col_count=col_count)
        for sg in range(col_count)
    ]
    return lax.switch(start % col_count, branches, packets)


def spread_pieces(piece, axis, owners, devices, pieces_axis):
    parts = devices // owners
    size = piece.shape[pieces_axis] // parts
    me = lax.axis_index(axis)
    sub = lax.slice_in_dim(piece, 0, size, axis=pieces_axis)
    for m in range(1, parts):
        part = lax.slice_in_dim(piece, m * size, (m + 1) * size, axis=pieces_axis)
        got = lax.ppermute(part, axis, [(k, m * owners + k) for k in range(owners)])
        sub = jnp.where(me // owners == m, got, sub)
    return lax.all_gather(sub, axis, axis=0, tiled=False), parts, size


def on_device(front_blocks, child_updates, child_map, row_count, col_count):
    row_index = lax.axis_index("row")
    col_index = lax.axis_index("col")
    slots_r, tile, slots_c, _ = front_blocks.shape
    child_count, kr_count, _, kc_count, _ = child_updates.shape
    home, shift, start, inv = decode_map(child_map, col_count)
    groups = home.shape[1]

    dense = []
    for i in range(child_count):
        with jax.named_scope("child_route"):
            x = child_updates[i].reshape(groups, kr_count // groups, tile, kc_count, tile)
            x = jnp.take(x, inv[i], axis=0)
            x = jnp.take(x, inv[i], axis=3)
            packets = jnp.transpose(x, (0, 3, 1, 2, 4))
            got = routed(packets, start[i], row_count, col_count)
            z = jnp.transpose(got, (0, 2, 3, 1, 4)).reshape(groups * 2, tile, groups, tile)
        with jax.named_scope("child_place"):
            qs = jnp.arange(groups)
            a_of = inv[i]
            s_of = shift[i, a_of]
            h_of = home[i, a_of]
            src = (start[i] + qs - row_index) % row_count
            per_home = col_count // row_count
            first = ((s_of - src) % col_count) // row_count
            row_slot = jnp.stack(
                [per_home * h_of + first, per_home * h_of + 1 - first], axis=1
            ).reshape(-1)
            col_slot = h_of
            row_src = jnp.sum(
                jnp.where(
                    row_slot[None, :] == jnp.arange(slots_r)[:, None],
                    jnp.arange(groups * 2)[None, :] + 1,
                    0,
                ),
                axis=1,
            ) - 1
            row_src = jnp.where(row_src < 0, groups * 2, row_src)
            col_src = jnp.sum(
                jnp.where(
                    col_slot[None, :] == jnp.arange(slots_c)[:, None],
                    jnp.arange(groups)[None, :] + 1,
                    0,
                ),
                axis=1,
            ) - 1
            col_src = jnp.where(col_src < 0, groups, col_src)
            zp = jnp.concatenate([z, jnp.zeros((1, tile, groups, tile), z.dtype)], axis=0)
            zp = jnp.take(zp, row_src, axis=0)
            zp = jnp.concatenate([zp, jnp.zeros((slots_r, tile, 1, tile), z.dtype)], axis=2)
            dense.append(jnp.take(zp, col_src, axis=2))

    with jax.named_scope("assemble"):
        assembled = front_blocks
        for d in dense:
            assembled = assembled + d.astype(jnp.float32)
        height = slots_r * tile
        breadth = slots_c * tile
        a2 = assembled.reshape(height, breadth)

    local_rows = jnp.arange(height, dtype=jnp.int32)
    row_global = (local_rows // tile * row_count + row_index) * tile + local_rows % tile
    local_cols = jnp.arange(breadth, dtype=jnp.int32)
    col_global = (local_cols // tile * col_count + col_index) * tile + local_cols % tile
    owners = PD // tile

    with jax.named_scope("gather_diagonal"):
        g, parts, size = spread_pieces(a2[0:tile, 0:tile], "col", owners, col_count, 0)
        g = g.reshape(parts, owners, size, tile).transpose(0, 2, 1, 3)
        strip = g.reshape(tile, PD)
        g, parts, size = spread_pieces(strip, "row", owners, row_count, 0)
        g = g.reshape(parts, owners, size, PD).transpose(1, 0, 2, 3)
        diag = g.reshape(PD, PD)
    with jax.named_scope("gather_panel_rows"):
        g, parts, size = spread_pieces(a2[:, 0:tile], "col", owners, col_count, 0)
        g = g.reshape(parts, owners, size, tile).transpose(0, 2, 1, 3)
        g_rows = g.reshape(height, PD)
    with jax.named_scope("gather_panel_cols"):
        g, parts, size = spread_pieces(a2[0:tile, :], "row", owners, row_count, 0)
        g = g.reshape(parts, owners, size, breadth).transpose(1, 0, 2, 3)
        g_cols = g.reshape(PD, breadth)

    with jax.named_scope("factor_diagonal"):
        factor, w = blocked_factor(diag, tile)

    def panel_rows(block, at):
        solved = jnp.dot(block, w, precision=lax.Precision.HIGH)
        inside = lax.dynamic_slice_in_dim(factor, jnp.minimum(at, owners - 1) * tile, tile, axis=0)
        head = jnp.where(at < owners, inside, solved[0:tile])
        return lax.dynamic_update_slice_in_dim(solved, head, 0, axis=0)

    with jax.named_scope("panel_factors"):
        pr = panel_rows(g_rows, row_index)
        pc = panel_rows(g_cols.T, col_index)

    with jax.named_scope("trailing_update"):
        out = a2 - jnp.dot(pr, pc.T, precision=lax.Precision.HIGH)
        own = lax.dynamic_slice_in_dim(pr, jnp.minimum(col_index, owners - 1) * tile, tile, axis=1)
        first = jnp.where(col_index < owners, own, out[:, 0:tile])
        out = lax.dynamic_update_slice_in_dim(out, first, 0, axis=1)
        top = out[0:tile]
        top = jnp.where((row_index < owners) & (col_global >= PD)[None, :], 0.0, top)
        out = lax.dynamic_update_slice_in_dim(out, top, 0, axis=0)
    return out.reshape(slots_r, tile, slots_c, tile)


def blocked_factor(matrix, size):
    count = matrix.shape[0] // size
    eye = jnp.eye(size, dtype=matrix.dtype)
    matrix = 0.5 * (matrix + matrix.T)
    blocks = [[matrix[i * size : (i + 1) * size, k * size : (k + 1) * size] for k in range(count)] for i in range(count)]
    low = [[None] * count for _ in range(count)]
    inv = [[None] * count for _ in range(count)]
    for k in range(count):
        low[k][k] = lax.linalg.cholesky(blocks[k][k], symmetrize_input=False)
        inv[k][k] = lax.linalg.triangular_solve(low[k][k], eye, left_side=True, lower=True)
        if k + 1 < count:
            below = jnp.concatenate([blocks[i][k] for i in range(k + 1, count)], axis=0)
            solved = jnp.dot(below, inv[k][k].T, precision=HI)
            for n, i in enumerate(range(k + 1, count)):
                low[i][k] = solved[n * size : (n + 1) * size]
            rest = jnp.dot(solved, solved.T, precision=HI)
            for n, i in enumerate(range(k + 1, count)):
                for m, j in enumerate(range(k + 1, count)):
                    blocks[i][j] = blocks[i][j] - rest[n * size : (n + 1) * size, m * size : (m + 1) * size]
    for j in range(count):
        for i in range(j + 1, count):
            acc = sum(jnp.dot(low[i][k], inv[k][j], precision=HI) for k in range(j, i))
            inv[i][j] = -jnp.dot(inv[i][i], acc, precision=HI)
    zero = jnp.zeros((size, size), matrix.dtype)
    factor = jnp.concatenate(
        [jnp.concatenate([low[i][k] if k <= i else zero for k in range(count)], axis=1) for i in range(count)], axis=0
    )
    inverse = jnp.concatenate(
        [jnp.concatenate([inv[i][k] if k <= i else zero for k in range(count)], axis=1) for i in range(count)], axis=0
    )
    return factor, inverse.T


def solution(mesh):
    placed = (P(None, "row", None, "col"), P(None, None, "row", None, "col"), P())
    row_count = mesh.shape["row"]
    col_count = mesh.shape["col"]

    def body(front_blocks, child_updates, child_map):
        return on_device(front_blocks, child_updates, child_map, row_count, col_count)

    return jax.shard_map(
        body,
        mesh=mesh,
        in_specs=placed,
        out_specs=P(None, "row", None, "col"),
        check_vma=False,
    )
```

```python
import functools

import jax
import jax.numpy as jnp
from jax import lax
from jax.experimental import pallas as pl
from jax.experimental.pallas import tpu as pltpu
from jax.sharding import PartitionSpec as P

PW = 256
PANELS = 2
PD = 512
HI = lax.Precision.HIGHEST
MESH = pl.DeviceIdType.MESH


def decode_map(child_map, lanes):
    base = child_map[:, ::lanes]
    home = base // lanes
    shift = base % lanes
    groups = base.shape[1]
    prev = (shift - 1) % lanes
    has_prev = jnp.any(prev[:, :, None] == shift[:, None, :], axis=2)
    start = jnp.sum(jnp.where(has_prev, 0, shift), axis=1)
    order = (shift - start[:, None]) % lanes
    picks = order[:, :, None] == jnp.arange(groups)[None, None, :]
    inv = jnp.sum(jnp.where(picks, jnp.arange(groups)[None, :, None], 0), axis=1)
    return home, shift, start, inv


def route_kernel(sigma, groups, row_count, col_count, pk_ref, out_ref, send_sem, recv_sem):
    row_at = lax.axis_index("row")
    col_at = lax.axis_index("col")
    sig_r = sigma % row_count
    targets = []
    for qr in range(groups):
        to_row = lax.rem(sig_r + qr - row_at + row_count, row_count)
        for qc in range(groups):
            to_col = lax.rem(sigma + qc - col_at + col_count, col_count)
            mine = (to_row == row_at) & (to_col == col_at)
            targets.append((qr, qc, to_row, to_col, mine))
    barrier = pltpu.get_barrier_semaphore()
    for qr, qc, to_row, to_col, mine in targets:

        @pl.when(jnp.logical_not(mine))
        def _():
            pl.semaphore_signal(barrier, 1, device_id=(to_row, to_col), device_id_type=MESH)

    peers = sum(jnp.logical_not(t[4]).astype(jnp.int32) for t in targets)
    pl.semaphore_wait(barrier, peers)

    copies = []
    for n, (qr, qc, to_row, to_col, mine) in enumerate(targets):
        remote = pltpu.make_async_remote_copy(
            src_ref=pk_ref.at[qr, qc],
            dst_ref=out_ref.at[qr, qc],
            send_sem=send_sem.at[n],
            recv_sem=recv_sem.at[n],
            device_id=(to_row, to_col),
            device_id_type=MESH,
        )
        local = pltpu.make_async_copy(pk_ref.at[qr, qc], out_ref.at[qr, qc], recv_sem.at[n])
        copies.append((remote, local, mine))

        @pl.when(jnp.logical_not(mine))
        def _():
            remote.start()

        @pl.when(mine)
        def _():
            local.start()

    for remote, local, mine in copies:

        @pl.when(jnp.logical_not(mine))
        def _():
            remote.wait()

        @pl.when(mine)
        def _():
            local.wait()


def route_call(packets, sigma, row_count, col_count):
    groups = packets.shape[0]
    count = groups * groups
    return pl.pallas_call(
        functools.partial(route_kernel, sigma, groups, row_count, col_count),
        out_shape=jax.ShapeDtypeStruct(packets.shape, packets.dtype),
        in_specs=[pl.BlockSpec(memory_space=pl.ANY)],
        out_specs=pl.BlockSpec(memory_space=pl.ANY),
        scratch_shapes=[pltpu.SemaphoreType.DMA((count,)), pltpu.SemaphoreType.DMA((count,))],
        compiler_params=pltpu.CompilerParams(collective_id=sigma, has_side_effects=True),
        name=f"route_{sigma}",
    )(packets)


def routed(packets, start, row_count, col_count):
    branches = [
        functools.partial(route_call, sigma=sg, row_count=row_count, col_count=col_count)
        for sg in range(col_count)
    ]
    return lax.switch(start % col_count, branches, packets)


def spread_pieces(piece, axis, owners, devices, pieces_axis):
    parts = devices // owners
    size = piece.shape[pieces_axis] // parts
    me = lax.axis_index(axis)
    sub = lax.slice_in_dim(piece, 0, size, axis=pieces_axis)
    for m in range(1, parts):
        part = lax.slice_in_dim(piece, m * size, (m + 1) * size, axis=pieces_axis)
        got = lax.ppermute(part, axis, [(k, m * owners + k) for k in range(owners)])
        sub = jnp.where(me // owners == m, got, sub)
    return lax.all_gather(sub, axis, axis=0, tiled=False), parts, size


def on_device(front_blocks, child_updates, child_map, row_count, col_count):
    row_index = lax.axis_index("row")
    col_index = lax.axis_index("col")
    slots_r, tile, slots_c, _ = front_blocks.shape
    child_count, kr_count, _, kc_count, _ = child_updates.shape
    home, shift, start, inv = decode_map(child_map, col_count)
    groups = home.shape[1]

    dense = []
    for i in range(child_count):
        with jax.named_scope("child_route"):
            x = child_updates[i].reshape(groups, kr_count // groups, tile, kc_count, tile)
            x = jnp.take(x, inv[i], axis=0, mode="clip")
            x = jnp.take(x, inv[i], axis=3, mode="clip")
            packets = jnp.transpose(x, (0, 3, 1, 2, 4))
            got = routed(packets, start[i], row_count, col_count)
            z = jnp.transpose(got, (0, 2, 3, 1, 4)).reshape(groups * 2, tile, groups, tile)
        with jax.named_scope("child_place"):
            qs = jnp.arange(groups)
            a_of = inv[i]
            s_of = shift[i, a_of]
            h_of = home[i, a_of]
            src = (start[i] + qs - row_index) % row_count
            per_home = col_count // row_count
            first = ((s_of - src) % col_count) // row_count
            row_slot = jnp.stack(
                [per_home * h_of + first, per_home * h_of + 1 - first], axis=1
            ).reshape(-1)
            col_slot = h_of
            row_src = jnp.sum(
                jnp.where(
                    row_slot[None, :] == jnp.arange(slots_r)[:, None],
                    jnp.arange(groups * 2)[None, :] + 1,
                    0,
                ),
                axis=1,
            ) - 1
            row_src = jnp.where(row_src < 0, groups * 2, row_src)
            col_src = jnp.sum(
                jnp.where(
                    col_slot[None, :] == jnp.arange(slots_c)[:, None],
                    jnp.arange(groups)[None, :] + 1,
                    0,
                ),
                axis=1,
            ) - 1
            col_src = jnp.where(col_src < 0, groups, col_src)
            zp = jnp.concatenate([z, jnp.zeros((1, tile, groups, tile), z.dtype)], axis=0)
            zp = jnp.take(zp, row_src, axis=0, mode="clip")
            zp = jnp.concatenate([zp, jnp.zeros((slots_r, tile, 1, tile), z.dtype)], axis=2)
            dense.append(jnp.take(zp, col_src, axis=2, mode="clip"))

    with jax.named_scope("assemble"):
        assembled = front_blocks
        for d in dense:
            assembled = assembled + d.astype(jnp.float32)
        height = slots_r * tile
        breadth = slots_c * tile
        a2 = assembled.reshape(height, breadth)

    local_rows = jnp.arange(height, dtype=jnp.int32)
    row_global = (local_rows // tile * row_count + row_index) * tile + local_rows % tile
    local_cols = jnp.arange(breadth, dtype=jnp.int32)
    col_global = (local_cols // tile * col_count + col_index) * tile + local_cols % tile
    owners = PD // tile

    with jax.named_scope("gather_diagonal"):
        g, parts, size = spread_pieces(a2[0:tile, 0:tile], "col", owners, col_count, 0)
        g = g.reshape(parts, owners, size, tile).transpose(0, 2, 1, 3)
        strip = g.reshape(tile, PD)
        g, parts, size = spread_pieces(strip, "row", owners, row_count, 0)
        g = g.reshape(parts, owners, size, PD).transpose(1, 0, 2, 3)
        diag = g.reshape(PD, PD)
    with jax.named_scope("gather_panel_rows"):
        g, parts, size = spread_pieces(a2[:, 0:tile], "col", owners, col_count, 0)
        g = g.reshape(parts, owners, size, tile).transpose(0, 2, 1, 3)
        g_rows = g.reshape(height, PD)
    with jax.named_scope("gather_panel_cols"):
        g, parts, size = spread_pieces(a2[0:tile, :], "row", owners, row_count, 0)
        g = g.reshape(parts, owners, size, breadth).transpose(1, 0, 2, 3)
        g_cols = g.reshape(PD, breadth)

    with jax.named_scope("factor_diagonal"):
        factor, w = blocked_factor(diag, tile)

    def panel_rows(block, at):
        solved = jnp.dot(block, w, precision=lax.Precision.HIGH)
        inside = lax.dynamic_slice_in_dim(factor, jnp.minimum(at, owners - 1) * tile, tile, axis=0)
        head = jnp.where(at < owners, inside, solved[0:tile])
        return lax.dynamic_update_slice_in_dim(solved, head, 0, axis=0)

    with jax.named_scope("panel_factors"):
        pr = panel_rows(g_rows, row_index)
        pc = panel_rows(g_cols.T, col_index)

    with jax.named_scope("trailing_update"):
        out = a2 - jnp.dot(pr, pc.T, precision=lax.Precision.HIGH)
        own = lax.dynamic_slice_in_dim(pr, jnp.minimum(col_index, owners - 1) * tile, tile, axis=1)
        first = jnp.where(col_index < owners, own, out[:, 0:tile])
        out = lax.dynamic_update_slice_in_dim(out, first, 0, axis=1)
        top = out[0:tile]
        top = jnp.where((row_index < owners) & (col_global >= PD)[None, :], 0.0, top)
        out = lax.dynamic_update_slice_in_dim(out, top, 0, axis=0)
    return out.reshape(slots_r, tile, slots_c, tile)


def blocked_factor(matrix, size):
    count = matrix.shape[0] // size
    eye = jnp.eye(size, dtype=matrix.dtype)
    matrix = 0.5 * (matrix + matrix.T)
    blocks = [[matrix[i * size : (i + 1) * size, k * size : (k + 1) * size] for k in range(count)] for i in range(count)]
    low = [[None] * count for _ in range(count)]
    inv = [[None] * count for _ in range(count)]
    for k in range(count):
        low[k][k] = lax.linalg.cholesky(blocks[k][k], symmetrize_input=False)
        inv[k][k] = lax.linalg.triangular_solve(low[k][k], eye, left_side=True, lower=True)
        if k + 1 < count:
            below = jnp.concatenate([blocks[i][k] for i in range(k + 1, count)], axis=0)
            solved = jnp.dot(below, inv[k][k].T, precision=HI)
            for n, i in enumerate(range(k + 1, count)):
                low[i][k] = solved[n * size : (n + 1) * size]
            rest = jnp.dot(solved, solved.T, precision=HI)
            for n, i in enumerate(range(k + 1, count)):
                for m, j in enumerate(range(k + 1, count)):
                    blocks[i][j] = blocks[i][j] - rest[n * size : (n + 1) * size, m * size : (m + 1) * size]
    for j in range(count):
        for i in range(j + 1, count):
            acc = sum(jnp.dot(low[i][k], inv[k][j], precision=HI) for k in range(j, i))
            inv[i][j] = -jnp.dot(inv[i][i], acc, precision=HI)
    zero = jnp.zeros((size, size), matrix.dtype)
    factor = jnp.concatenate(
        [jnp.concatenate([low[i][k] if k <= i else zero for k in range(count)], axis=1) for i in range(count)], axis=0
    )
    inverse = jnp.concatenate(
        [jnp.concatenate([inv[i][k] if k <= i else zero for k in range(count)], axis=1) for i in range(count)], axis=0
    )
    return factor, inverse.T


def solution(mesh):
    placed = (P(None, "row", None, "col"), P(None, None, "row", None, "col"), P())
    row_count = mesh.shape["row"]
    col_count = mesh.shape["col"]

    def body(front_blocks, child_updates, child_map):
        return on_device(front_blocks, child_updates, child_map, row_count, col_count)

    return jax.shard_map(
        body,
        mesh=mesh,
        in_specs=placed,
        out_specs=P(None, "row", None, "col"),
        check_vma=False,
    )
```

```python
import functools

import jax
import jax.numpy as jnp
from jax import lax
from jax.experimental import pallas as pl
from jax.experimental.pallas import tpu as pltpu
from jax.sharding import PartitionSpec as P

PW = 256
PANELS = 2
PD = 512
HI = lax.Precision.HIGHEST
MESH = pl.DeviceIdType.MESH


def decode_map(child_map, lanes):
    base = child_map[:, ::lanes]
    home = base // lanes
    shift = base % lanes
    groups = base.shape[1]
    prev = (shift - 1) % lanes
    has_prev = jnp.any(prev[:, :, None] == shift[:, None, :], axis=2)
    start = jnp.sum(jnp.where(has_prev, 0, shift), axis=1)
    order = (shift - start[:, None]) % lanes
    picks = order[:, :, None] == jnp.arange(groups)[None, None, :]
    inv = jnp.sum(jnp.where(picks, jnp.arange(groups)[None, :, None], 0), axis=1)
    return home, shift, start, inv


def route_kernel(sigma, groups, row_count, col_count, pk_ref, out_ref, send_sem, recv_sem):
    row_at = lax.axis_index("row")
    col_at = lax.axis_index("col")
    sig_r = sigma % row_count
    targets = []
    for qr in range(groups):
        to_row = lax.rem(sig_r + qr - row_at + row_count, row_count)
        for qc in range(groups):
            to_col = lax.rem(sigma + qc - col_at + col_count, col_count)
            mine = (to_row == row_at) & (to_col == col_at)
            targets.append((qr, qc, to_row, to_col, mine))
    barrier = pltpu.get_barrier_semaphore()
    for qr, qc, to_row, to_col, mine in targets:

        @pl.when(jnp.logical_not(mine))
        def _():
            pl.semaphore_signal(barrier, 1, device_id=(to_row, to_col), device_id_type=MESH)

    peers = sum(jnp.logical_not(t[4]).astype(jnp.int32) for t in targets)
    pl.semaphore_wait(barrier, peers)

    copies = []
    for n, (qr, qc, to_row, to_col, mine) in enumerate(targets):
        remote = pltpu.make_async_remote_copy(
            src_ref=pk_ref.at[qr, qc],
            dst_ref=out_ref.at[qr, qc],
            send_sem=send_sem.at[n],
            recv_sem=recv_sem.at[n],
            device_id=(to_row, to_col),
            device_id_type=MESH,
        )
        local = pltpu.make_async_copy(pk_ref.at[qr, qc], out_ref.at[qr, qc], recv_sem.at[n])
        copies.append((remote, local, mine))

        @pl.when(jnp.logical_not(mine))
        def _():
            remote.start()

        @pl.when(mine)
        def _():
            local.start()

    for remote, local, mine in copies:

        @pl.when(jnp.logical_not(mine))
        def _():
            remote.wait()

        @pl.when(mine)
        def _():
            local.wait()


def route_call(packets, sigma, row_count, col_count):
    groups = packets.shape[0]
    count = groups * groups
    return pl.pallas_call(
        functools.partial(route_kernel, sigma, groups, row_count, col_count),
        out_shape=jax.ShapeDtypeStruct(packets.shape, packets.dtype),
        in_specs=[pl.BlockSpec(memory_space=pl.ANY)],
        out_specs=pl.BlockSpec(memory_space=pl.ANY),
        scratch_shapes=[pltpu.SemaphoreType.DMA((count,)), pltpu.SemaphoreType.DMA((count,))],
        compiler_params=pltpu.CompilerParams(collective_id=sigma, has_side_effects=True),
        name=f"route_{sigma}",
    )(packets)


def routed(packets, start, row_count, col_count):
    branches = [
        functools.partial(route_call, sigma=sg, row_count=row_count, col_count=col_count)
        for sg in range(col_count)
    ]
    return lax.switch(start % col_count, branches, packets)


def spread_pieces(piece, axis, owners, devices, pieces_axis):
    parts = devices // owners
    size = piece.shape[pieces_axis] // parts
    me = lax.axis_index(axis)
    sub = lax.slice_in_dim(piece, 0, size, axis=pieces_axis)
    for m in range(1, parts):
        part = lax.slice_in_dim(piece, m * size, (m + 1) * size, axis=pieces_axis)
        got = lax.ppermute(part, axis, [(k, m * owners + k) for k in range(owners)])
        sub = jnp.where(me // owners == m, got, sub)
    return lax.all_gather(sub, axis, axis=0, tiled=False), parts, size


def on_device(front_blocks, child_updates, child_map, row_count, col_count):
    row_index = lax.axis_index("row")
    col_index = lax.axis_index("col")
    slots_r, tile, slots_c, _ = front_blocks.shape
    child_count, kr_count, _, kc_count, _ = child_updates.shape
    home, shift, start, inv = decode_map(child_map, col_count)
    groups = home.shape[1]

    dense = []
    for i in range(child_count):
        with jax.named_scope("child_route"):
            x = child_updates[i].reshape(groups, kr_count // groups, tile, kc_count, tile)
            x = jnp.take(x, inv[i], axis=0, mode="clip")
            x = jnp.take(x, inv[i], axis=3, mode="clip")
            packets = jnp.transpose(x, (0, 3, 1, 2, 4))
            got = routed(packets, start[i], row_count, col_count)
            z = jnp.transpose(got, (0, 2, 3, 1, 4)).reshape(groups * 2, tile, groups, tile)
        with jax.named_scope("child_place"):
            qs = jnp.arange(groups)
            a_of = inv[i]
            s_of = shift[i, a_of]
            h_of = home[i, a_of]
            src = (start[i] + qs - row_index) % row_count
            per_home = col_count // row_count
            first = ((s_of - src) % col_count) // row_count
            row_slot = jnp.stack(
                [per_home * h_of + first, per_home * h_of + 1 - first], axis=1
            ).reshape(-1)
            col_slot = h_of
            row_src = jnp.sum(
                jnp.where(
                    row_slot[None, :] == jnp.arange(slots_r)[:, None],
                    jnp.arange(groups * 2)[None, :] + 1,
                    0,
                ),
                axis=1,
            ) - 1
            row_src = jnp.where(row_src < 0, groups * 2, row_src)
            col_src = jnp.sum(
                jnp.where(
                    col_slot[None, :] == jnp.arange(slots_c)[:, None],
                    jnp.arange(groups)[None, :] + 1,
                    0,
                ),
                axis=1,
            ) - 1
            col_src = jnp.where(col_src < 0, groups, col_src)
            zp = jnp.concatenate([z, jnp.zeros((1, tile, groups, tile), z.dtype)], axis=0)
            zp = jnp.take(zp, row_src, axis=0, mode="clip")
            zp = jnp.concatenate([zp, jnp.zeros((slots_r, tile, 1, tile), z.dtype)], axis=2)
            dense.append(jnp.take(zp, col_src, axis=2, mode="clip"))

    with jax.named_scope("assemble"):
        assembled = front_blocks
        for d in dense:
            assembled = assembled + d.astype(jnp.float32)
        height = slots_r * tile
        breadth = slots_c * tile
        a2 = assembled.reshape(height, breadth)

    local_rows = jnp.arange(height, dtype=jnp.int32)
    row_global = (local_rows // tile * row_count + row_index) * tile + local_rows % tile
    local_cols = jnp.arange(breadth, dtype=jnp.int32)
    col_global = (local_cols // tile * col_count + col_index) * tile + local_cols % tile
    owners = PD // tile

    with jax.named_scope("gather_diagonal"):
        g, parts, size = spread_pieces(a2[0:tile, 0:tile], "col", owners, col_count, 0)
        g = g.reshape(parts, owners, size, tile).transpose(0, 2, 1, 3)
        strip = g.reshape(tile, PD)
        g, parts, size = spread_pieces(strip, "row", owners, row_count, 0)
        g = g.reshape(parts, owners, size, PD).transpose(1, 0, 2, 3)
        diag = g.reshape(PD, PD)
    with jax.named_scope("gather_panel_rows"):
        g, parts, size = spread_pieces(a2[:, 0:tile], "col", owners, col_count, 0)
        g = g.reshape(parts, owners, size, tile).transpose(0, 2, 1, 3)
        g_rows = g.reshape(height, PD)
    with jax.named_scope("gather_panel_cols"):
        g, parts, size = spread_pieces(a2[0:tile, :], "row", owners, row_count, 0)
        g = g.reshape(parts, owners, size, breadth).transpose(1, 0, 2, 3)
        g_cols = g.reshape(PD, breadth)

    with jax.named_scope("factor_diagonal"):
        factor, w = blocked_factor(diag, tile)

    def panel_rows(block, at):
        solved = jnp.dot(block, w, precision=lax.Precision.HIGH)
        inside = lax.dynamic_slice_in_dim(factor, jnp.minimum(at, owners - 1) * tile, tile, axis=0)
        head = jnp.where(at < owners, inside, solved[0:tile])
        return lax.dynamic_update_slice_in_dim(solved, head, 0, axis=0)

    with jax.named_scope("panel_factors"):
        pr = panel_rows(g_rows, row_index)
        pc = panel_rows(g_cols.T, col_index)

    with jax.named_scope("trailing_update"):
        out = a2 - jnp.dot(pr, pc.T, precision=lax.Precision.HIGH)
        own = lax.dynamic_slice_in_dim(pr, jnp.minimum(col_index, owners - 1) * tile, tile, axis=1)
        first = jnp.where(col_index < owners, own, out[:, 0:tile])
        out = lax.dynamic_update_slice_in_dim(out, first, 0, axis=1)
        top = out[0:tile]
        top = jnp.where((row_index < owners) & (col_global >= PD)[None, :], 0.0, top)
        out = lax.dynamic_update_slice_in_dim(out, top, 0, axis=0)
    return out.reshape(slots_r, tile, slots_c, tile)


def blocked_factor(matrix, size):
    count = matrix.shape[0] // size
    eye = jnp.eye(size, dtype=matrix.dtype)
    matrix = 0.5 * (matrix + matrix.T)
    blocks = [[matrix[i * size : (i + 1) * size, k * size : (k + 1) * size] for k in range(count)] for i in range(count)]
    low = [[None] * count for _ in range(count)]
    inv = [[None] * count for _ in range(count)]
    for k in range(count):
        low[k][k] = lax.linalg.cholesky(blocks[k][k], symmetrize_input=False)
        inv[k][k] = lax.linalg.triangular_solve(low[k][k], eye, left_side=True, lower=True)
        if k + 1 < count:
            below = jnp.concatenate([blocks[i][k] for i in range(k + 1, count)], axis=0)
            solved = jnp.dot(below, inv[k][k].T, precision=lax.Precision.HIGH)
            for n, i in enumerate(range(k + 1, count)):
                low[i][k] = solved[n * size : (n + 1) * size]
            rest = jnp.dot(solved, solved.T, precision=lax.Precision.HIGH)
            for n, i in enumerate(range(k + 1, count)):
                for m, j in enumerate(range(k + 1, count)):
                    blocks[i][j] = blocks[i][j] - rest[n * size : (n + 1) * size, m * size : (m + 1) * size]
    for j in range(count):
        for i in range(j + 1, count):
            acc = sum(jnp.dot(low[i][k], inv[k][j], precision=lax.Precision.HIGH) for k in range(j, i))
            inv[i][j] = -jnp.dot(inv[i][i], acc, precision=lax.Precision.HIGH)
    zero = jnp.zeros((size, size), matrix.dtype)
    factor = jnp.concatenate(
        [jnp.concatenate([low[i][k] if k <= i else zero for k in range(count)], axis=1) for i in range(count)], axis=0
    )
    inverse = jnp.concatenate(
        [jnp.concatenate([inv[i][k] if k <= i else zero for k in range(count)], axis=1) for i in range(count)], axis=0
    )
    return factor, inverse.T


def solution(mesh):
    placed = (P(None, "row", None, "col"), P(None, None, "row", None, "col"), P())
    row_count = mesh.shape["row"]
    col_count = mesh.shape["col"]

    def body(front_blocks, child_updates, child_map):
        return on_device(front_blocks, child_updates, child_map, row_count, col_count)

    return jax.shard_map(
        body,
        mesh=mesh,
        in_specs=placed,
        out_specs=P(None, "row", None, "col"),
        check_vma=False,
    )
```
